128 devices in a mesh: pitch: 16 (over x, z), span: 8 (over y, core).
Axes of the slice: x: 4, y: 4, z: 4, core: 2. Of those that a mesh axis runs over, the one named last changes fastest.
Arguments:
- stator_state: float32 [5, 16, 512, 2048], P(None, None, 'span', 'pitch'), may hold values from -6 to 6
- rotor_state: float32 [5, 16, 512, 2048], P(None, None, 'span', 'pitch'), may hold values from -6 to 6
- jacobians: float32 [3, 5, 5], replicated, may hold values from -2.5 to 2.5
- field_mix: float32 [5, 5], replicated, may hold values from -2.5 to 2.5
- mode_blend: float32 [5, 2048], replicated, may hold values from 0.1 to 0.9
- rotor_offset: int32 [1], replicated, may hold values from 0 to 2047
Outputs:
- stator_next: float32 [5, 16, 512, 2048], P(None, None, 'span', 'pitch')
- rotor_next: float32 [5, 16, 512, 2048], P(None, None, 'span', 'pitch')
The draws below stay inside these ranges and needn't reach their ends.
Inputs may be any that keep to these rules, and one draw needn't show every extreme that they name: `rotor_offset`: the rotor's rotation against the stator, in whole pitch cells.
All inputs are finite; a program needn't handle non-finite values.
Results may differ from the reference program's by a relative error of at most 0.0001.
Values sent between devices are 32-bit elements; how exact they have to be, the bound alone decides.
A program may use at most 192 MiB of HBM per device.

```python
import jax
import jax.numpy as jnp
from jax import lax

NP = 2048
FIELDS = 5
AX = 16
NR = 512


def block_levels(key, extent, pieces, least, top_value):
    def one(position, shards_of):
        heights = jax.random.uniform(jax.random.fold_in(jax.random.fold_in(key, 6), position), (shards_of,), jnp.float32, least / len(pieces), top_value / len(pieces))
        return jnp.repeat(jnp.exp(heights), extent[position] // shards_of).reshape((-1,) + (1,) * (len(extent) - position - 1))

    factor_of = one(*pieces[0])
    for cut in pieces[1:]:
        factor_of = factor_of * one(*cut)
    return factor_of


def scatter_about(stream_key, shape, spread, reach, cuts=(), kind=jnp.bfloat16):
    level = block_levels(stream_key, shape, cuts, -0.22, 0.18) if cuts else 1.0
    array = jax.random.normal(stream_key, shape, jnp.float32) * spread * level
    return jnp.minimum(jnp.maximum(array, -reach), reach).astype(kind)


def setup_inputs(seed: int = 0) -> dict:
    key_list = jax.random.split(jax.random.key(seed), 7)
    return {
        "stator_state": scatter_about(key_list[0], (FIELDS, AX, NR, NP), 1.0, 6.0, ((2, 8), (3, 16)), jnp.float32),
        "rotor_state": scatter_about(key_list[1], (FIELDS, AX, NR, NP), 1.0, 6.0, ((2, 8), (3, 16)), jnp.float32),
        "jacobians": scatter_about(key_list[2], (3, FIELDS, FIELDS), FIELDS ** -0.5, 2.5, (), jnp.float32),
        "field_mix": scatter_about(key_list[3], (FIELDS, FIELDS), FIELDS ** -0.5, 2.5, (), jnp.float32),
        "mode_blend": jnp.clip(jax.random.uniform(key_list[4], (FIELDS, NP), jnp.float32, 0.1, 0.9), 0.1, 0.9),
        "rotor_offset": jax.random.randint(key_list[5], (1,), 0, NP).astype(jnp.int32),
    }


time_step = 0.5
damping = 1.0 / 32.0


def hartley(planes):
    spectrum = jnp.fft.fft(planes, axis=-1)
    return jnp.real(spectrum) - jnp.imag(spectrum)


def block_update(state, before, after, jacobians):
    extended = jnp.concatenate([before, state, after], axis=1)
    extended = jnp.pad(extended, ((0, 0), (0, 0), (2, 2), (0, 0)))
    extended = jnp.pad(extended, ((0, 0), (0, 0), (0, 0), (2, 2)), mode="wrap")

    def one_layer(layer):
        window = lax.dynamic_slice_in_dim(extended, layer, 5, 1)
        centre = window[:, 2, 2:-2, 2:-2]
        neighbours = (
            (window[:, 3, 2:-2, 2:-2], window[:, 1, 2:-2, 2:-2], window[:, 4, 2:-2, 2:-2], window[:, 0, 2:-2, 2:-2]),
            (window[:, 2, 3:-1, 2:-2], window[:, 2, 1:-3, 2:-2], window[:, 2, 4:, 2:-2], window[:, 2, :-4, 2:-2]),
            (window[:, 2, 2:-2, 3:-1], window[:, 2, 2:-2, 1:-3], window[:, 2, 2:-2, 4:], window[:, 2, 2:-2, :-4]),
        )
        totals = jnp.zeros_like(centre)
        for course in range(3):
            plus_one, minus_one, plus_two, minus_two = neighbours[course]
            slopes = 0.5 * (plus_one - minus_one)
            totals = totals - jnp.einsum("fg,gsp->fsp", jacobians[course], slopes, precision=lax.Precision.HIGHEST)
            totals = totals - damping * (plus_two - 4.0 * plus_one + 6.0 * centre - 4.0 * minus_one + minus_two)
        return totals

    changes = lax.map(one_layer, jnp.arange(state.shape[1], dtype=jnp.int32))
    return state + time_step * jnp.moveaxis(changes, 0, 1)


def reference(stator_state, rotor_state, jacobians, field_mix, mode_blend, rotor_offset):
    offset = rotor_offset[0]
    stator_planes = jnp.stack([stator_state[:, -1], stator_state[:, -2]], axis=1)
    rotor_planes = rotor_state[:, 0:2]
    stator_modes = hartley(stator_planes)
    rotor_modes = hartley(jnp.roll(rotor_planes, offset, axis=-1))
    blend = mode_blend[:, None, None, :]
    stator_blend = blend * rotor_modes + (1.0 - blend) * stator_modes
    rotor_blend = blend * stator_modes + (1.0 - blend) * rotor_modes
    stator_back = hartley(stator_blend) / NP
    rotor_back = jnp.roll(hartley(rotor_blend) / NP, -offset, axis=-1)
    stator_ghost = jnp.einsum("fg,glrp->flrp", field_mix, stator_back, precision=lax.Precision.HIGHEST)
    rotor_ghost = jnp.einsum("fg,glrp->flrp", field_mix, rotor_back, precision=lax.Precision.HIGHEST)
    no_inflow = jnp.zeros((FIELDS, 2, NR, NP), jnp.float32)
    stator_next = block_update(stator_state, no_inflow, stator_ghost, jacobians)
    rotor_next = block_update(rotor_state, rotor_ghost[:, ::-1], no_inflow, jacobians)
    return stator_next, rotor_next
```

```python
import math

import jax
import jax.numpy as jnp
import ml_dtypes
import numpy as np
from jax import lax
from jax.experimental import pallas as pl
from jax.experimental.pallas import tpu as pltpu
from jax.sharding import PartitionSpec as P

NP = 2048
FIELDS = 5
AX = 16
ROWS = 64
LANES = 128
TILES = 16
MESH = pl.DeviceIdType.MESH
f32 = jnp.float32
bf16 = jnp.bfloat16

time_step = 0.5
damping = 1.0 / 32.0


def transform_tables():
    q = np.arange(LANES)
    w = 2.0 * np.pi / LANES

    def cas(m):
        angle = w * (m % LANES)
        return np.cos(angle) + np.sin(angle)

    first, second = np.outer(q, q), np.outer(q, q + 1)
    table = np.block([[cas(first), cas(second)], [-cas(-first), cas(-second)]])

    def parts(array):
        array = array.astype(np.float32)
        high = array.astype(ml_dtypes.bfloat16)
        low = (array - high.astype(np.float32)).astype(ml_dtypes.bfloat16)
        return np.stack([high, low])

    psi = 2.0 * np.pi * np.outer(np.arange(9), q) / NP
    twiddle = np.stack([np.cos(psi), np.sin(psi)]).astype(np.float32)
    return parts(table), parts(table.T / NP), twiddle[:, :, None, :]


def cosine(m):
    return math.cos(2.0 * math.pi * (m % 16) / 16)


def sine(m):
    return math.sin(2.0 * math.pi * (m % 16) / 16)


def weighted(terms):
    total = None
    for weight, value in terms:
        if abs(weight) < 1e-9:
            continue
        if abs(weight - 1.0) < 1e-9:
            total = value if total is None else total + value
        elif abs(weight + 1.0) < 1e-9:
            total = -value if total is None else total - value
        else:
            total = weight * value if total is None else total + weight * value
    return total


def forward_16(x):
    e = [None] + [x[p] + x[16 - p] for p in range(1, 8)]
    o = [None] + [x[p] - x[16 - p] for p in range(1, 8)]
    x_even, x_odd = x[0] + x[8], x[0] - x[8]
    ee = [None] + [e[p] + e[8 - p] for p in range(1, 4)]
    eo = [None] + [e[p] - e[8 - p] for p in range(1, 4)]
    oo = [None] + [o[p] + o[8 - p] for p in range(1, 4)]
    oe = [None] + [o[p] - o[8 - p] for p in range(1, 4)]
    cs, ss = [], []
    for c in range(9):
        if c % 2 == 0:
            cs.append(weighted([(1.0, x_even), (cosine(4 * c), e[4])] + [(cosine(p * c), ee[p]) for p in range(1, 4)]))
            ss.append(weighted([(sine(p * c), oe[p]) for p in range(1, 4)]) if 0 < c < 8 else None)
        else:
            cs.append(weighted([(1.0, x_odd)] + [(cosine(p * c), eo[p]) for p in range(1, 4)]))
            ss.append(weighted([(sine(4 * c), o[4])] + [(sine(p * c), oo[p]) for p in range(1, 4)]))
    return cs, ss


def inverse_16(cs, ss):
    x = [None] * 16
    x[0] = weighted([(1.0, v) for v in cs])
    x[8] = weighted([((-1.0) ** c, v) for c, v in enumerate(cs)])
    for p in range(1, 5):
        ev = weighted([(1.0, cs[0]), (cosine(8 * p), cs[8])] + [(cosine(p * c), cs[c]) for c in range(2, 8, 2)])
        eo = weighted([(cosine(p * c), cs[c]) for c in range(1, 8, 2)])
        ov = weighted([(sine(p * c), ss[c]) for c in range(2, 8, 2)])
        oo = weighted([(sine(p * c), ss[c]) for c in range(1, 8, 2)])
        if p == 4:
            x[4], x[12] = ev + oo, ev - oo
            continue
        x[p] = (ev + eo) + (ov + oo)
        x[16 - p] = (ev + eo) - (ov + oo)
        x[8 - p] = (ev - eo) + (oo - ov)
        x[8 + p] = (ev - eo) - (oo - ov)
    return x


def split_dot(values, table_ref):
    high = values.astype(bf16)
    low = (values - high.astype(f32)).astype(bf16)

    def dot(left, right):
        return jnp.dot(left, right, preferred_element_type=f32)

    return dot(high, table_ref[0]) + dot(low, table_ref[0]) + dot(high, table_ref[1])


def interface_kernel(
    off_ref, st_ref, ro_ref, blend_ref, table_ref, back_ref, twiddle_ref,
    ghost_ref, pitch_ref, span_ref,
    state, planes, spectrum, blends, turned, outgoing, pitch_pack, span_pack,
    load_sem, own_sem, row_send, row_recv, back_send, back_recv, halo_send, halo_recv,
):
    me = lax.axis_index("pitch")
    span = lax.axis_index("span")
    left, right = lax.rem(me + 15, 16), lax.rem(me + 1, 16)
    below, above = lax.rem(span + 7, 8), lax.rem(span + 1, 8)
    states = (st_ref, ro_ref)

    def load(s, f):
        return pltpu.make_async_copy(states[s].at[f], state.at[s, f], load_sem.at[s, f])

    def row_block(s, target):
        layer, block = target // 8, target % 8
        axial = 15 - layer if s == 0 else layer
        rows = pl.ds(pl.multiple_of(8 * block, 8), 8)
        return states[s].at[:, axial, rows, :]

    def own_rows(s):
        return pltpu.make_async_copy(row_block(s, me), planes.at[s, me], own_sem.at[s])

    for s in range(2):
        own_rows(s).start()
    for s in range(2):
        for f in range(FIELDS):
            load(s, f).start()

    barrier = pltpu.get_barrier_semaphore()

    def greet(j, carry):
        pl.semaphore_signal(barrier, inc=1, device_id={"pitch": lax.rem(me + j, 16)}, device_id_type=MESH)
        return carry

    lax.fori_loop(1, 16, greet, 0)
    for other in (below, above):
        pl.semaphore_signal(barrier, inc=1, device_id={"span": other}, device_id_type=MESH)
    pl.semaphore_wait(barrier, 17)

    def row_copy(s, target, source):
        return pltpu.make_async_remote_copy(
            src_ref=row_block(s, target), dst_ref=planes.at[s, source],
            send_sem=row_send.at[s, target], recv_sem=row_recv.at[s, source],
            device_id={"pitch": target}, device_id_type=MESH,
        )

    def send_rows(j, carry):
        target = lax.rem(me + j, 16)
        for s in range(2):
            row_copy(s, target, me).start()
        return carry

    lax.fori_loop(1, 16, send_rows, 0)

    def halo_copy(slot, src, dst, where):
        return pltpu.make_async_remote_copy(
            src_ref=src, dst_ref=dst, send_sem=halo_send.at[slot], recv_sem=halo_recv.at[slot],
            device_id=where, device_id_type=MESH,
        )

    halos = (
        halo_copy(0, span_pack.at[0], span_ref.at[0], {"span": above}),
        halo_copy(1, span_pack.at[1], span_ref.at[1], {"span": below}),
        halo_copy(2, pitch_pack, pitch_ref.at[0], {"pitch": right}),
        halo_copy(3, pitch_pack, pitch_ref.at[1], {"pitch": left}),
    )

    lane = lax.broadcasted_iota(jnp.int32, (8, LANES), 1)
    row = lax.broadcasted_iota(jnp.int32, (8, LANES), 0)
    for s in range(2):
        for f in range(FIELDS):
            load(s, f).wait()

        def pack(m, carry):
            f, first = m // 4, 4 * (m % 4)
            edge = jnp.zeros((8, LANES), f32)
            low = jnp.zeros((8, LANES), f32)
            high = jnp.zeros((8, LANES), f32)
            for j in range(4):
                for t in range(8):
                    n = 8 * j + t
                    value = state[s, f, first + j, 8 * t:8 * t + 8, :]
                    edge = jnp.where(lane // 4 == n, pltpu.roll(value, (2 + 4 * n) % LANES, 1), edge)
                    if t == 0:
                        low = jnp.where(row // 2 == j, pltpu.roll(value, 2 * j, 0) if j else value, low)
                    if t == 7:
                        shift = (2 * j + 2) % 8
                        high = jnp.where(row // 2 == j, pltpu.roll(value, shift, 0) if shift else value, high)
            pitch_pack[s, m] = edge
            span_pack[0, s, m] = high
            span_pack[1, s, m] = low
            return carry

        lax.fori_loop(0, 20, pack, 0)
    for copy in halos:
        copy.start()

    nothing = jnp.zeros((8, LANES), f32)
    for c in range(9):
        for f in range(FIELDS):
            blends[c, f, :, 0:LANES] = jnp.broadcast_to(blend_ref[c, f:f + 1, :], (8, LANES))
            other = jnp.broadcast_to(blend_ref[16 - c, f:f + 1, :], (8, LANES)) if 0 < c < 8 else nothing
            blends[c, f, :, LANES:] = other

    offset = off_ref[0]
    shift, hop = lax.rem(offset, LANES), offset // LANES

    for s in range(2):
        own_rows(s).wait()

    def wait_rows(j, carry):
        source = lax.rem(me + j, 16)
        for s in range(2):
            row_copy(s, source, source).wait_recv()
        return carry

    lax.fori_loop(1, 16, wait_rows, 0)

    def forward(f, carry):
        for t in range(TILES):
            turned[t] = pltpu.roll(planes[1, t, f], shift, 1)
        x = []
        for t in range(TILES):
            near = turned[lax.rem(t + 16 - hop, 16)]
            far = turned[lax.rem(t + 15 - hop, 16)]
            x.append(jnp.where(lane >= shift, near, far) - planes[0, t, f])
        cs, ss = forward_16(x)
        for c in range(9):
            cosines, sines = twiddle_ref[0, c], twiddle_ref[1, c]
            if c == 0:
                real, imaginary = cs[0], nothing
            elif c == 8:
                real, imaginary = cs[8] * cosines, -(cs[8] * sines)
            else:
                real = cs[c] * cosines - ss[c] * sines
                imaginary = -(cs[c] * sines + ss[c] * cosines)
            spectrum[c, f, :, 0:LANES] = real
            spectrum[c, f, :, LANES:] = imaginary
        return carry

    lax.fori_loop(0, FIELDS, forward, 0)
    modes = split_dot(spectrum[...].reshape(9 * 40, 256), table_ref)
    modes = modes * blends[...].reshape(9 * 40, 256)
    spectrum[...] = split_dot(modes, back_ref).reshape(9, FIELDS, 8, 256)

    def inverse(f, carry):
        cs, ss = [], []
        for c in range(9):
            cosines, sines = twiddle_ref[0, c], twiddle_ref[1, c]
            real, imaginary = spectrum[c, f, :, 0:LANES], spectrum[c, f, :, LANES:]
            cs.append(real * cosines - imaginary * sines)
            ss.append(-(real * sines + imaginary * cosines))
        x = inverse_16(cs, ss)
        for t in range(TILES):
            outgoing[t, 0, f] = x[t]
            turned[t] = pltpu.roll(x[t], lax.rem(LANES - shift, LANES), 1)
        for t in range(TILES):
            near = turned[lax.rem(t + hop, 16)]
            far = turned[lax.rem(t + hop + 1, 16)]
            outgoing[t, 1, f] = jnp.where(lane < LANES - shift, near, far)
        return carry

    lax.fori_loop(0, FIELDS, inverse, 0)

    def back_copy(target, source):
        return pltpu.make_async_remote_copy(
            src_ref=outgoing.at[target], dst_ref=ghost_ref.at[source],
            send_sem=back_send.at[target], recv_sem=back_recv.at[source],
            device_id={"pitch": target}, device_id_type=MESH,
        )

    def send_back(j, carry):
        back_copy(lax.rem(me + j, 16), me).start()
        return carry

    lax.fori_loop(1, 16, send_back, 0)
    own_back = pltpu.make_async_copy(outgoing.at[me], ghost_ref.at[me], own_sem.at[0])
    own_back.start()
    for copy in halos:
        copy.wait()
    own_back.wait()

    def finish(j, carry):
        other = lax.rem(me + j, 16)
        for s in range(2):
            row_copy(s, other, me).wait_send()
        back_copy(other, me).wait_send()
        back_copy(other, other).wait_recv()
        return carry

    lax.fori_loop(1, 16, finish, 0)


def interface(offset, stator, rotor, blend):
    forward_table, back_table, twiddle = transform_tables()
    whole = pl.BlockSpec(memory_space=pltpu.VMEM)
    anywhere = pl.BlockSpec(memory_space=pl.ANY)
    dma = pltpu.SemaphoreType.DMA
    return pl.pallas_call(
        interface_kernel,
        name="interface",
        out_shape=(
            jax.ShapeDtypeStruct((16, 2, FIELDS, 8, LANES), f32),
            jax.ShapeDtypeStruct((2, 2, 20, 8, LANES), f32),
            jax.ShapeDtypeStruct((2, 2, 20, 8, LANES), f32),
        ),
        in_specs=[pl.BlockSpec(memory_space=pltpu.SMEM), anywhere, anywhere, whole, whole, whole, whole],
        out_specs=(anywhere, anywhere, anywhere),
        scratch_shapes=[
            pltpu.VMEM((2, FIELDS, AX, ROWS, LANES), f32),
            pltpu.VMEM((2, 16, FIELDS, 8, LANES), f32),
            pltpu.VMEM((9, FIELDS, 8, 256), f32),
            pltpu.VMEM((9, FIELDS, 8, 256), f32),
            pltpu.VMEM((16, 8, LANES), f32),
            pltpu.VMEM((16, 2, FIELDS, 8, LANES), f32),
            pltpu.VMEM((2, 20, 8, LANES), f32),
            pltpu.VMEM((2, 2, 20, 8, LANES), f32),
            dma((2, FIELDS)), dma((2,)), dma((2, 16)), dma((2, 16)), dma((16,)), dma((16,)), dma((4,)), dma((4,)),
        ],
        compiler_params=pltpu.CompilerParams(
            collective_id=0, has_side_effects=True, vmem_limit_bytes=48 << 20
        ),
    )(offset, stator, rotor, blend, forward_table, back_table, twiddle)


def update_kernel(
    jac_ref, mix_ref, st_ref, ro_ref, ghost_ref, pitch_ref, span_ref,
    st_out, ro_out,
    cells, result, ghosts, edges, rims, weights,
    load_sem, small_sem, store_sem,
):
    span = lax.axis_index("span")
    states, outs = (st_ref, ro_ref), (st_out, ro_out)

    def load(s, f):
        return pltpu.make_async_copy(states[s].at[f], cells.at[s, f, pl.ds(2, AX), pl.ds(8, ROWS)], load_sem.at[s, f])

    small = (
        pltpu.make_async_copy(pitch_ref, edges, small_sem.at[0]),
        pltpu.make_async_copy(span_ref, rims, small_sem.at[1]),
        pltpu.make_async_copy(ghost_ref, ghosts, small_sem.at[2]),
    )
    for copy in small:
        copy.start()
    for s in range(2):
        for f in range(FIELDS):
            load(s, f).start()

    for d in range(3):
        for f in range(FIELDS):
            for g in range(FIELDS):
                weights[(d * FIELDS + g) * FIELDS + f] = jnp.full((8, LANES), -0.5 * time_step * jac_ref[d, f, g], f32)
    for f in range(FIELDS):
        for t in range(8):
            for a in range(2):
                cells[0, f, a, 8 + 8 * t:16 + 8 * t, :] = jnp.zeros((8, LANES), f32)
                cells[1, f, 18 + a, 8 + 8 * t:16 + 8 * t, :] = jnp.zeros((8, LANES), f32)
    for copy in small:
        copy.wait()
    lane = lax.broadcasted_iota(jnp.int32, (8, LANES), 1)
    keep_low = jnp.where(span == 0, 0.0, 1.0).astype(f32)
    keep_high = jnp.where(span == 7, 0.0, 1.0).astype(f32)
    for s in range(2):

        def unpack(m, carry):
            f, first = m // 4, 4 * (m % 4)
            low = rims[0, s, m] * keep_low
            high = rims[1, s, m] * keep_high
            for j in range(4):
                cells[s, f, 2 + first + j, 6:8, :] = low[2 * j:2 * j + 2, :]
                cells[s, f, 2 + first + j, 72:74, :] = high[2 * j:2 * j + 2, :]
            edges[0, s, m] = jnp.where(lane % 4 < 2, edges[0, s, m], edges[1, s, m])
            return carry

        lax.fori_loop(0, 20, unpack, 0)

    for s in range(2):
        for f in range(FIELDS):
            load(s, f).wait()

        def fill(block, carry):
            rows = pl.ds(pl.multiple_of(8 + 8 * block, 8), 8)
            for layer in range(2):
                planes = []
                for g in range(FIELDS):
                    change = ghosts[8 * layer + block, s, g]
                    planes.append(cells[s, g, 17 - layer if s == 0 else 2 + layer, rows, :] + (change if s == 0 else -change))
                for f in range(FIELDS):
                    total = mix_ref[f, 0] * planes[0]
                    for g in range(1, FIELDS):
                        total = total + mix_ref[f, g] * planes[g]
                    cells[s, f, 18 + layer if s == 0 else 1 - layer, rows, :] = total
            return carry

        lax.fori_loop(0, 8, fill, 0)

        def store(a):
            return pltpu.make_async_copy(result.at[s, :, a], outs[s].at[:, a], store_sem.at[s, a])

        def layer_update(a, carry):
            for half in range(2):
                start = 8 + 32 * half
                sums = []
                slopes = []
                for g in range(FIELDS):

                    def get(axial, radial):
                        return cells[s, g, a + 2 + axial, start + radial:start + radial + 32, :].reshape(4, 8, LANES)

                    centre = get(0, 0)
                    pack = edges[0, s, 4 * g + a // 4]
                    base = 126 - 32 * lax.rem(a, 4)
                    halo = jnp.stack([
                        pltpu.roll(pack, lax.rem(base - 4 * (4 * half + t) + 2 * LANES, LANES), 1) for t in range(4)
                    ])
                    right_1 = pltpu.roll(jnp.where(lane == 0, halo, centre), LANES - 1, 2)
                    right_2 = pltpu.roll(jnp.where(lane < 2, halo, centre), LANES - 2, 2)
                    left_1 = pltpu.roll(jnp.where(lane == LANES - 1, halo, centre), 1, 2)
                    left_2 = pltpu.roll(jnp.where(lane >= LANES - 2, halo, centre), 2, 2)
                    ahead, behind = get(1, 0), get(-1, 0)
                    up, down = get(0, 1), get(0, -1)
                    near = (ahead + behind) + (up + down) + (right_1 + left_1)
                    far = (get(2, 0) + get(-2, 0)) + (get(0, 2) + get(0, -2)) + (right_2 + left_2)
                    scale = time_step * damping
                    sums.append((1.0 - 18.0 * scale) * centre + (4.0 * scale) * near - scale * far)
                    slopes.append((ahead - behind, up - down, right_1 - left_1))
                for d in range(3):
                    for g in range(FIELDS):
                        for f in range(FIELDS):
                            sums[f] = sums[f] + weights[(d * FIELDS + g) * FIELDS + f] * slopes[g][d]
                for f in range(FIELDS):
                    result[s, f, a, 32 * half:32 * half + 32, :] = sums[f].reshape(32, LANES)
            store(a).start()
            return carry

        lax.fori_loop(0, AX, layer_update, 0)

    for s in range(2):
        for a in range(AX):
            pltpu.make_async_copy(result.at[s, :, a], outs[s].at[:, a], store_sem.at[s, a]).wait()


def update(jacobians, field_mix, stator, rotor, ghosts, pitch_halo, span_halo):
    anywhere = pl.BlockSpec(memory_space=pl.ANY)
    scalars = pl.BlockSpec(memory_space=pltpu.SMEM)
    dma = pltpu.SemaphoreType.DMA
    shape = jax.ShapeDtypeStruct((FIELDS, AX, ROWS, LANES), f32)
    return pl.pallas_call(
        update_kernel,
        name="update",
        out_shape=(shape, shape),
        in_specs=[scalars, scalars] + [anywhere] * 5,
        out_specs=(anywhere, anywhere),
        scratch_shapes=[
            pltpu.VMEM((2, FIELDS, AX + 4, ROWS + 16, LANES), f32),
            pltpu.VMEM((2, FIELDS, AX, ROWS, LANES), f32),
            pltpu.VMEM((16, 2, FIELDS, 8, LANES), f32),
            pltpu.VMEM((2, 2, 20, 8, LANES), f32),
            pltpu.VMEM((2, 2, 20, 8, LANES), f32),
            pltpu.VMEM((75, 8, LANES), f32),
            dma((2, FIELDS)), dma((3,)), dma((2, AX)),
        ],
        compiler_params=pltpu.CompilerParams(vmem_limit_bytes=48 << 20),
    )(jacobians, field_mix, stator, rotor, ghosts, pitch_halo, span_halo)


def shards(stator_state, rotor_state, jacobians, field_mix, mode_blend, rotor_offset):
    blend = mode_blend.reshape(FIELDS, LANES, 16).transpose(2, 0, 1)
    ghosts, pitch_halo, span_halo = interface(rotor_offset, stator_state, rotor_state, blend)
    return update(jacobians, field_mix, stator_state, rotor_state, ghosts, pitch_halo, span_halo)


def solution(mesh):
    in_specs = (P(None, None, "span", "pitch"), P(None, None, "span", "pitch"), P(), P(), P(), P())
    out_specs = (P(None, None, "span", "pitch"), P(None, None, "span", "pitch"))
    return jax.shard_map(shards, mesh=mesh, in_specs=in_specs, out_specs=out_specs, check_vma=False)
```

```python
import math

import jax
import jax.numpy as jnp
import ml_dtypes
import numpy as np
from jax import lax
from jax.experimental import pallas as pl
from jax.experimental.pallas import tpu as pltpu
from jax.sharding import PartitionSpec as P

NP = 2048
FIELDS = 5
AX = 16
ROWS = 64
LANES = 128
TILES = 16
MESH = pl.DeviceIdType.MESH
f32 = jnp.float32
bf16 = jnp.bfloat16

time_step = 0.5
damping = 1.0 / 32.0


def transform_tables():
    q = np.arange(LANES)
    w = 2.0 * np.pi / LANES

    def cas(m):
        angle = w * (m % LANES)
        return np.cos(angle) + np.sin(angle)

    first, second = np.outer(q, q), np.outer(q, q + 1)
    table = np.block([[cas(first), cas(second)], [-cas(-first), cas(-second)]])

    def parts(array):
        array = array.astype(np.float32)
        high = array.astype(ml_dtypes.bfloat16)
        low = (array - high.astype(np.float32)).astype(ml_dtypes.bfloat16)
        return np.stack([high, low])

    psi = 2.0 * np.pi * np.outer(np.arange(9), q) / NP
    twiddle = np.stack([np.cos(psi), np.sin(psi)]).astype(np.float32)
    return parts(table), parts(table.T / NP), twiddle[:, :, None, :]


def cosine(m):
    return math.cos(2.0 * math.pi * (m % 16) / 16)


def sine(m):
    return math.sin(2.0 * math.pi * (m % 16) / 16)


def weighted(terms):
    total = None
    for weight, value in terms:
        if abs(weight) < 1e-9:
            continue
        if abs(weight - 1.0) < 1e-9:
            total = value if total is None else total + value
        elif abs(weight + 1.0) < 1e-9:
            total = -value if total is None else total - value
        else:
            total = weight * value if total is None else total + weight * value
    return total


def forward_16(x):
    e = [None] + [x[p] + x[16 - p] for p in range(1, 8)]
    o = [None] + [x[p] - x[16 - p] for p in range(1, 8)]
    x_even, x_odd = x[0] + x[8], x[0] - x[8]
    ee = [None] + [e[p] + e[8 - p] for p in range(1, 4)]
    eo = [None] + [e[p] - e[8 - p] for p in range(1, 4)]
    oo = [None] + [o[p] + o[8 - p] for p in range(1, 4)]
    oe = [None] + [o[p] - o[8 - p] for p in range(1, 4)]
    cs, ss = [], []
    for c in range(9):
        if c % 2 == 0:
            cs.append(weighted([(1.0, x_even), (cosine(4 * c), e[4])] + [(cosine(p * c), ee[p]) for p in range(1, 4)]))
            ss.append(weighted([(sine(p * c), oe[p]) for p in range(1, 4)]) if 0 < c < 8 else None)
        else:
            cs.append(weighted([(1.0, x_odd)] + [(cosine(p * c), eo[p]) for p in range(1, 4)]))
            ss.append(weighted([(sine(4 * c), o[4])] + [(sine(p * c), oo[p]) for p in range(1, 4)]))
    return cs, ss


def inverse_16(cs, ss):
    x = [None] * 16
    x[0] = weighted([(1.0, v) for v in cs])
    x[8] = weighted([((-1.0) ** c, v) for c, v in enumerate(cs)])
    for p in range(1, 5):
        ev = weighted([(1.0, cs[0]), (cosine(8 * p), cs[8])] + [(cosine(p * c), cs[c]) for c in range(2, 8, 2)])
        eo = weighted([(cosine(p * c), cs[c]) for c in range(1, 8, 2)])
        ov = weighted([(sine(p * c), ss[c]) for c in range(2, 8, 2)])
        oo = weighted([(sine(p * c), ss[c]) for c in range(1, 8, 2)])
        if p == 4:
            x[4], x[12] = ev + oo, ev - oo
            continue
        x[p] = (ev + eo) + (ov + oo)
        x[16 - p] = (ev + eo) - (ov + oo)
        x[8 - p] = (ev - eo) + (oo - ov)
        x[8 + p] = (ev - eo) - (oo - ov)
    return x


def split_dot(values, table_ref):
    high = values.astype(bf16)
    low = (values - high.astype(f32)).astype(bf16)

    def dot(left, right):
        return jnp.dot(left, right, preferred_element_type=f32)

    return dot(high, table_ref[0]) + dot(low, table_ref[0]) + dot(high, table_ref[1])


def section_kernel(
    off_ref, st_ref, ro_ref, blend_hbm, jac_hbm, mix_hbm, table_hbm, back_hbm, twiddle_hbm, band_hbm,
    partial, ghost_ref, weights, mixes,
    cells, planes, spectrum, blends, turned, outgoing, pitch_pack, pitch_recv, span_pack, span_recv,
    bent_a, bent_b, edge_fix, permuted, blend_v, jac_v, mix_v, table_ref, back_ref, twiddle_ref, band_ref,
    load_sem, own_sem, row_send, row_recv, back_send, back_recv, halo_send, halo_recv, small_sem,
):
    me = lax.axis_index("pitch")
    span = lax.axis_index("span")
    left, right = lax.rem(me + 15, 16), lax.rem(me + 1, 16)
    below, above = lax.rem(span + 7, 8), lax.rem(span + 1, 8)
    states = (st_ref, ro_ref)

    def load(s, f):
        return pltpu.make_async_copy(states[s].at[f], cells.at[s, f, pl.ds(2, AX), pl.ds(8, ROWS)], load_sem.at[s, f])

    def row_block(s, target):
        layer, block = target // 8, target % 8
        axial = 15 - layer if s == 0 else layer
        rows = pl.ds(pl.multiple_of(8 * block, 8), 8)
        return states[s].at[:, axial, rows, :]

    def own_rows(s):
        return pltpu.make_async_copy(row_block(s, me), planes.at[s, me], own_sem.at[s])

    barrier = pltpu.get_barrier_semaphore()

    def greet(j, carry):
        pl.semaphore_signal(barrier, inc=1, device_id={"pitch": lax.rem(me + j, 16)}, device_id_type=MESH)
        return carry

    lax.fori_loop(1, 16, greet, 0)
    for other in (below, above):
        pl.semaphore_signal(barrier, inc=1, device_id={"span": other}, device_id_type=MESH)

    smalls = [
        pltpu.make_async_copy(source, target, small_sem.at[i])
        for i, (source, target) in enumerate((
            (blend_hbm, blend_v), (jac_hbm, jac_v), (mix_hbm, mix_v),
            (table_hbm, table_ref), (back_hbm, back_ref), (twiddle_hbm, twiddle_ref), (band_hbm, band_ref),
        ))
    ]
    for s in range(2):
        own_rows(s).start()
    for s in range(2):
        for f in range(FIELDS):
            load(s, f).start()
    for copy in smalls:
        copy.start()

    lane = lax.broadcasted_iota(jnp.int32, (8, LANES), 1)
    row = lax.broadcasted_iota(jnp.int32, (8, LANES), 0)
    group = lane % 4
    nothing = jnp.zeros((8, LANES), f32)
    for s in range(2):
        for f in range(FIELDS):
            for t in range(8):
                for a in (0, 1, 18, 19):
                    cells[s, f, a, 8 + 8 * t:16 + 8 * t, :] = nothing

    pl.semaphore_wait(barrier, 17)

    def row_copy(s, target, source):
        return pltpu.make_async_remote_copy(
            src_ref=row_block(s, target), dst_ref=planes.at[s, source],
            send_sem=row_send.at[s, target], recv_sem=row_recv.at[s, source],
            device_id={"pitch": target}, device_id_type=MESH,
        )

    def send_rows(j, carry):
        target = lax.rem(me + j, 16)
        for s in range(2):
            row_copy(s, target, me).start()
        return carry

    lax.fori_loop(1, 16, send_rows, 0)

    def halo_copy(slot, src, dst, where):
        return pltpu.make_async_remote_copy(
            src_ref=src, dst_ref=dst, send_sem=halo_send.at[slot], recv_sem=halo_recv.at[slot],
            device_id=where, device_id_type=MESH,
        )

    to_above = halo_copy(0, span_pack.at[0], span_recv.at[0], {"span": above})
    to_below = halo_copy(1, span_pack.at[1], span_recv.at[1], {"span": below})
    to_right = halo_copy(2, pitch_pack.at[0], pitch_recv.at[0], {"pitch": right})
    to_left = halo_copy(3, pitch_pack.at[1], pitch_recv.at[1], {"pitch": left})

    for s in range(2):
        for f in range(FIELDS):
            load(s, f).wait()

        def pack(pair, carry):
            found = []
            for half in range(2):
                m = 2 * pair + half
                f, first = m // 4, 2 + 4 * (m % 4)
                edge = jnp.zeros((8, LANES), f32)
                low = jnp.zeros((8, LANES), f32)
                high = jnp.zeros((8, LANES), f32)
                for j in range(4):
                    for t in range(8):
                        n = 8 * j + t
                        value = cells[s, f, first + j, 8 + 8 * t:16 + 8 * t, :]
                        edge = jnp.where(lane // 4 == n, pltpu.roll(value, (2 + 4 * n) % LANES, 1), edge)
                        if t == 0:
                            low = jnp.where(row // 2 == j, pltpu.roll(value, 2 * j, 0) if j else value, low)
                        if t == 7:
                            shift = (2 * j + 2) % 8
                            high = jnp.where(row // 2 == j, pltpu.roll(value, shift, 0) if shift else value, high)
                span_pack[0, s, m] = high
                span_pack[1, s, m] = low
                found.append(edge)
            pitch_pack[0, s, pair] = jnp.where(group < 2, found[0], pltpu.roll(found[1], 2, 1))
            pitch_pack[1, s, pair] = jnp.where(group < 2, pltpu.roll(found[0], LANES - 2, 1), found[1])
            return carry

        lax.fori_loop(0, 10, pack, 0)
    for copy in (to_above, to_below, to_right, to_left):
        copy.start()

    for copy in smalls:
        copy.wait()
    for d in range(3):
        for f in range(FIELDS):
            for g in range(FIELDS):
                value = jnp.broadcast_to(jac_v[f, d:d + 1, g:g + 1], (8, LANES))
                weights[(d * FIELDS + g) * FIELDS + f] = (-0.5 * time_step) * value
    for f in range(FIELDS):
        for g in range(FIELDS):
            mixes[f * FIELDS + g] = jnp.broadcast_to(mix_v[f:f + 1, g:g + 1], (8, LANES))

    spare = jnp.zeros((3, LANES), f32)
    blend_rows = jnp.concatenate(
        [part for t in range(TILES) for part in (blend_v[:, LANES * t:LANES * t + LANES], spare)], axis=0
    )
    source_lane = lax.broadcasted_iota(jnp.int32, (LANES, LANES), 0)
    target_lane = lax.broadcasted_iota(jnp.int32, (LANES, LANES), 1)
    chosen = (8 * (source_lane % 16) + source_lane // 16 == target_lane).astype(f32)
    permuted[...] = jnp.dot(
        blend_rows, chosen, precision=lax.Precision.HIGHEST, preferred_element_type=f32
    ).reshape(TILES, 8, LANES)

    def mode_row(k):
        total = nothing
        for t in range(TILES):
            shift = (8 * (t - k)) % LANES
            value = permuted[t]
            total = jnp.where(lane // 8 == t, pltpu.roll(value, shift, 1) if shift else value, total)
        return total

    for c in range(9):
        near = mode_row(c)
        other = mode_row(16 - c) if 0 < c < 8 else nothing
        for f in range(FIELDS):
            blends[c, f, :, 0:LANES] = jnp.broadcast_to(near[f:f + 1, :], (8, LANES))
            blends[c, f, :, LANES:] = jnp.broadcast_to(other[f:f + 1, :], (8, LANES))

    def base_ghosts(block, carry):
        rows = pl.ds(pl.multiple_of(8 + 8 * block, 8), 8)
        for s in range(2):
            for layer in range(2):
                kept = [cells[s, g, 17 - layer if s == 0 else 2 + layer, rows, :] for g in range(FIELDS)]
                for f in range(FIELDS):
                    total = mixes[f * FIELDS] * kept[0]
                    for g in range(1, FIELDS):
                        total = total + mixes[f * FIELDS + g] * kept[g]
                    cells[s, f, 18 + layer if s == 0 else 1 - layer, rows, :] = total
        return carry

    lax.fori_loop(0, 8, base_ghosts, 0)

    offset = off_ref[0]
    shift, hop = lax.rem(offset, LANES), offset // LANES

    for s in range(2):
        own_rows(s).wait()

    def wait_rows(j, carry):
        source = lax.rem(me + j, 16)
        for s in range(2):
            row_copy(s, source, source).wait_recv()
        return carry

    lax.fori_loop(1, 16, wait_rows, 0)

    def forward(f, carry):
        for t in range(TILES):
            turned[t] = pltpu.roll(planes[1, t, f], shift, 1)
        x = []
        for t in range(TILES):
            near = turned[lax.rem(t + 16 - hop, 16)]
            far = turned[lax.rem(t + 15 - hop, 16)]
            x.append(jnp.where(lane >= shift, near, far) - planes[0, t, f])
        cs, ss = forward_16(x)
        for c in range(9):
            cosines, sines = twiddle_ref[0, c], twiddle_ref[1, c]
            if c == 0:
                real, imaginary = cs[0], nothing
            elif c == 8:
                real, imaginary = cs[8] * cosines, -(cs[8] * sines)
            else:
                real = cs[c] * cosines - ss[c] * sines
                imaginary = -(cs[c] * sines + ss[c] * cosines)
            spectrum[c, f, :, 0:LANES] = real
            spectrum[c, f, :, LANES:] = imaginary
        return carry

    lax.fori_loop(0, FIELDS, forward, 0)
    modes = split_dot(spectrum[...].reshape(9 * 40, 256), table_ref)
    modes = modes * blends[...].reshape(9 * 40, 256)
    spectrum[...] = split_dot(modes, back_ref).reshape(9, FIELDS, 8, 256)

    def inverse(f, carry):
        cs, ss = [], []
        for c in range(9):
            cosines, sines = twiddle_ref[0, c], twiddle_ref[1, c]
            real, imaginary = spectrum[c, f, :, 0:LANES], spectrum[c, f, :, LANES:]
            cs.append(real * cosines - imaginary * sines)
            ss.append(-(real * sines + imaginary * cosines))
        x = inverse_16(cs, ss)
        for t in range(TILES):
            outgoing[t, 0, f] = x[t]
            turned[t] = pltpu.roll(x[t], lax.rem(LANES - shift, LANES), 1)
        for t in range(TILES):
            near = turned[lax.rem(t + hop, 16)]
            far = turned[lax.rem(t + hop + 1, 16)]
            outgoing[t, 1, f] = jnp.where(lane < LANES - shift, near, far)
        return carry

    lax.fori_loop(0, FIELDS, inverse, 0)

    def back_copy(target, source):
        return pltpu.make_async_remote_copy(
            src_ref=outgoing.at[target], dst_ref=ghost_ref.at[source],
            send_sem=back_send.at[target], recv_sem=back_recv.at[source],
            device_id={"pitch": target}, device_id_type=MESH,
        )

    def send_back(j, carry):
        back_copy(lax.rem(me + j, 16), me).start()
        return carry

    lax.fori_loop(1, 16, send_back, 0)
    own_back = pltpu.make_async_copy(outgoing.at[me], ghost_ref.at[me], own_sem.at[0])
    own_back.start()

    for copy in (to_above, to_below, to_right, to_left):
        copy.wait()
    keep_low = jnp.where(span == 0, 0.0, 1.0).astype(f32)
    keep_high = jnp.where(span == 7, 0.0, 1.0).astype(f32)
    scale = time_step * damping
    for s in range(2):

        def unpack(m, carry):
            f, first = m // 4, 4 * (m % 4)
            low = span_recv[0, s, m] * keep_low
            high = span_recv[1, s, m] * keep_high
            for j in range(4):
                cells[s, f, 2 + first + j, 6:8, :] = low[2 * j:2 * j + 2, :]
                cells[s, f, 2 + first + j, 72:74, :] = high[2 * j:2 * j + 2, :]
            return carry

        lax.fori_loop(0, 20, unpack, 0)

        def edges(quarter_pair, carry):
            total = [[None] * FIELDS, [None] * FIELDS]
            for g in range(FIELDS):
                from_left, from_right = pitch_recv[0, s, 2 * g + quarter_pair], pitch_recv[1, s, 2 * g + quarter_pair]
                for half in range(2):
                    if half == 0:
                        halo = jnp.where(group < 2, from_left, pltpu.roll(from_right, 2, 1))
                    else:
                        halo = jnp.where(group < 2, pltpu.roll(from_left, LANES - 2, 1), from_right)
                    plus_1, minus_1 = pltpu.roll(halo, LANES - 1, 1), pltpu.roll(halo, 1, 1)
                    plus_2, minus_2 = pltpu.roll(halo, LANES - 2, 1), pltpu.roll(halo, 2, 1)
                    slope = jnp.where(group == 1, plus_1, jnp.where(group == 2, -minus_1, 0.0))
                    smooth = jnp.where(group < 2, plus_2, minus_2) - 4.0 * jnp.where(
                        group == 1, plus_1, jnp.where(group == 2, minus_1, 0.0)
                    )
                    for f in range(FIELDS):
                        term = weights[(2 * FIELDS + g) * FIELDS + f] * slope
                        if f == g:
                            term = term - scale * smooth
                        total[half][f] = term if total[half][f] is None else total[half][f] + term
            for half in range(2):
                for f in range(FIELDS):
                    edge_fix[s, f, 2 * quarter_pair + half] = total[half][f]
            return carry

        lax.fori_loop(0, 2, edges, 0)

    rim = (lane < 2) | (lane >= LANES - 2)

    def bend(layer, target):
        s, a = layer // AX, layer % AX
        values = cells[s, :, a + 2, 8:8 + ROWS, :].reshape(FIELDS * ROWS, LANES)
        high = values.astype(bf16)
        low = (values - high.astype(f32)).astype(bf16)
        both = jnp.concatenate([high, low], axis=1)
        target[...] = jnp.dot(both, band_ref[...], preferred_element_type=f32).reshape(FIELDS, ROWS, 256)

    def advance(layer, bent):
        s, a = layer // AX, layer % AX
        for half in range(2):
            start = 8 + 32 * half
            sums = [None] * FIELDS
            for g in range(FIELDS):

                def get(axial, radial):
                    return cells[s, g, a + 2 + axial, start + radial:start + radial + 32, :].reshape(4, 8, LANES)

                ahead, behind = get(1, 0), get(-1, 0)
                up, down = get(0, 1), get(0, -1)
                near = (ahead + behind) + (up + down)
                far = (get(2, 0) + get(-2, 0)) + (get(0, 2) + get(0, -2))
                along = bent[g, 32 * half:32 * half + 32, 0:LANES].reshape(4, 8, LANES)
                own = bent[g, 32 * half:32 * half + 32, LANES:].reshape(4, 8, LANES)
                own = own + ((4.0 * scale) * near - scale * far)
                fix = edge_fix[s, g, a // 4]
                base = 126 - 32 * lax.rem(a, 4)
                own = own + jnp.stack([
                    jnp.where(rim, pltpu.roll(fix, lax.rem(base - 4 * (4 * half + t) + 2 * LANES, LANES), 1), 0.0)
                    for t in range(4)
                ])
                sums[g] = own if sums[g] is None else sums[g] + own
                for d, slope in enumerate((ahead - behind, up - down, along)):
                    for f in range(FIELDS):
                        term = weights[(d * FIELDS + g) * FIELDS + f] * slope
                        sums[f] = term if sums[f] is None else sums[f] + term
            for f in range(FIELDS):
                partial[s, f, a, 32 * half:32 * half + 32, :] = sums[f].reshape(32, LANES)

    bend(0, bent_a)

    def two_layers(i, carry):
        bend(2 * i + 1, bent_b)
        advance(2 * i, bent_a)
        bend(jnp.minimum(2 * i + 2, 2 * AX - 1), bent_a)
        advance(2 * i + 1, bent_b)
        return carry

    lax.fori_loop(0, AX, two_layers, 0)

    own_back.wait()

    def finish(j, carry):
        other = lax.rem(me + j, 16)
        for s in range(2):
            row_copy(s, other, me).wait_send()
        back_copy(other, me).wait_send()
        back_copy(other, other).wait_recv()
        return carry

    lax.fori_loop(1, 16, finish, 0)


def band_table():
    position = np.arange(LANES)
    scale = time_step * damping
    slope = np.zeros((LANES, LANES))
    smooth = np.zeros((LANES, LANES))
    for step, weight in ((1, 1.0), (-1, -1.0)):
        inside = position[(position + step >= 0) & (position + step < LANES)]
        slope[inside + step, inside] += weight
    for step, weight in ((0, 1.0 - 18.0 * scale), (1, 4.0 * scale), (-1, 4.0 * scale), (2, -scale), (-2, -scale)):
        inside = position[(position + step >= 0) & (position + step < LANES)]
        smooth[inside + step, inside] += weight
    table = np.concatenate([slope, smooth], axis=1)
    return np.concatenate([table, table], axis=0).astype(ml_dtypes.bfloat16)


def section(offset, stator, rotor, blend, jacobians, field_mix):
    forward_table, back_table, twiddle = transform_tables()
    whole = pl.BlockSpec(memory_space=pltpu.VMEM)
    anywhere = pl.BlockSpec(memory_space=pl.ANY)
    dma = pltpu.SemaphoreType.DMA
    return pl.pallas_call(
        section_kernel,
        name="section",
        out_shape=(
            pltpu.VMEM((2, FIELDS, AX, ROWS, LANES), f32),
            pltpu.VMEM((16, 2, FIELDS, 8, LANES), f32),
            pltpu.VMEM((75, 8, LANES), f32),
            pltpu.VMEM((25, 8, LANES), f32),
        ),
        in_specs=[pl.BlockSpec(memory_space=pltpu.SMEM)] + [pl.BlockSpec(memory_space=pltpu.HBM)] * 9,
        out_specs=(whole, whole, whole, whole),
        scratch_shapes=[
            pltpu.VMEM((2, FIELDS, AX + 4, ROWS + 16, LANES), f32),
            pltpu.VMEM((2, 16, FIELDS, 8, LANES), f32),
            pltpu.VMEM((9, FIELDS, 8, 256), f32),
            pltpu.VMEM((9, FIELDS, 8, 256), f32),
            pltpu.VMEM((16, 8, LANES), f32),
            pltpu.VMEM((16, 2, FIELDS, 8, LANES), f32),
            pltpu.VMEM((2, 2, 10, 8, LANES), f32),
            pltpu.VMEM((2, 2, 10, 8, LANES), f32),
            pltpu.VMEM((2, 2, 20, 8, LANES), f32),
            pltpu.VMEM((2, 2, 20, 8, LANES), f32),
            pltpu.VMEM((FIELDS, ROWS, 256), f32),
            pltpu.VMEM((FIELDS, ROWS, 256), f32),
            pltpu.VMEM((2, FIELDS, 4, 8, LANES), f32),
            pltpu.VMEM((TILES, 8, LANES), f32),
            pltpu.VMEM((FIELDS, NP), f32),
            pltpu.VMEM((FIELDS, 3, FIELDS), f32),
            pltpu.VMEM((FIELDS, FIELDS), f32),
            pltpu.VMEM((2, 256, 256), bf16),
            pltpu.VMEM((2, 256, 256), bf16),
            pltpu.VMEM((2, 9, 1, LANES), f32),
            pltpu.VMEM((256, 256), bf16),
            dma((2, FIELDS)), dma((2,)), dma((2, 16)), dma((2, 16)), dma((16,)), dma((16,)), dma((4,)), dma((4,)), dma((7,)),
        ],
        compiler_params=pltpu.CompilerParams(
            collective_id=0, has_side_effects=True, vmem_limit_bytes=32 << 20
        ),
    )(offset, *(
        pltpu.with_memory_space_constraint(jnp.asarray(x), pltpu.HBM)
        for x in (
            stator, rotor, blend, jacobians.transpose(1, 0, 2), field_mix,
            forward_table, back_table, twiddle, band_table(),
        )
    ))


def close_kernel(partial, ghosts, weights, mixes, st_out, ro_out, ends, store_sem, end_sem):
    outs = (st_out, ro_out)
    scale = time_step * damping
    copies = []
    for s in range(2):
        first = 0 if s == 0 else 2
        for f in range(FIELDS):
            copies.append(pltpu.make_async_copy(
                partial.at[s, f, pl.ds(first, AX - 2)], outs[s].at[f, pl.ds(first, AX - 2)], store_sem.at[s, f]
            ))
    for copy in copies:
        copy.start()

    for s in range(2):

        def fill(block, carry):
            rows = pl.ds(pl.multiple_of(8 * block, 8), 8)
            mixed = []
            for layer in range(2):
                parts = [ghosts[8 * layer + block, s, g] for g in range(FIELDS)]
                found = []
                for f in range(FIELDS):
                    total = mixes[f * FIELDS] * parts[0]
                    for g in range(1, FIELDS):
                        total = total + mixes[f * FIELDS + g] * parts[g]
                    found.append(total if s == 0 else -total)
                mixed.append(found)
            outer, inner = (15, 14) if s == 0 else (0, 1)
            for f in range(FIELDS):
                total = (4.0 * scale) * mixed[0][f] - scale * mixed[1][f]
                for g in range(FIELDS):
                    term = weights[g * FIELDS + f] * mixed[0][g]
                    total = total + term if s == 0 else total - term
                ends[s, f, outer % 2, rows, :] = partial[s, f, outer, rows, :] + total
                ends[s, f, inner % 2, rows, :] = partial[s, f, inner, rows, :] - scale * mixed[0][f]
            return carry

        lax.fori_loop(0, 8, fill, 0)
        last = pltpu.make_async_copy(ends.at[s], outs[s].at[:, pl.ds(14 if s == 0 else 0, 2)], end_sem.at[s])
        last.start()
        copies.append(last)
    for copy in copies:
        copy.wait()


def close(partial, ghosts, weights, mixes):
    anywhere = pl.BlockSpec(memory_space=pl.ANY)
    whole = pl.BlockSpec(memory_space=pltpu.VMEM)
    dma = pltpu.SemaphoreType.DMA
    shape = jax.ShapeDtypeStruct((FIELDS, AX, ROWS, LANES), f32)
    return pl.pallas_call(
        close_kernel,
        name="close",
        out_shape=(shape, shape),
        in_specs=[whole] * 4,
        out_specs=(anywhere, anywhere),
        scratch_shapes=[pltpu.VMEM((2, FIELDS, 2, ROWS, LANES), f32), dma((2, FIELDS)), dma((2,))],
        compiler_params=pltpu.CompilerParams(vmem_limit_bytes=8 << 20),
    )(partial, ghosts, weights, mixes)


def shards(stator_state, rotor_state, jacobians, field_mix, mode_blend, rotor_offset):
    parts = section(rotor_offset, stator_state, rotor_state, mode_blend, jacobians, field_mix)
    return close(*parts)


def solution(mesh):
    in_specs = (P(None, None, "span", "pitch"), P(None, None, "span", "pitch"), P(), P(), P(), P())
    out_specs = (P(None, None, "span", "pitch"), P(None, None, "span", "pitch"))
    return jax.shard_map(shards, mesh=mesh, in_specs=in_specs, out_specs=out_specs, check_vma=False)
```

```python
import math

import jax
import jax.numpy as jnp
import ml_dtypes
import numpy as np
from jax import lax
from jax.experimental import pallas as pl
from jax.experimental.pallas import tpu as pltpu
from jax.sharding import PartitionSpec as P

NP = 2048
FIELDS = 5
AX = 16
ROWS = 64
LANES = 128
TILES = 16
MESH = pl.DeviceIdType.MESH
EARLY = 12
BEFORE = (12,)
CHUNKS = ((0, 5),)
ORDER = (
    (2, 2), (2, 3), (3, 2), (2, 1), (1, 2), (2, 0), (0, 2), (3, 1), (1, 3), (3, 3), (1, 1), (3, 0), (0, 3), (1, 0), (0, 1),
)
f32 = jnp.float32
bf16 = jnp.bfloat16

time_step = 0.5
damping = 1.0 / 32.0


def transform_tables():
    q = np.arange(LANES)
    w = 2.0 * np.pi / LANES

    def cas(m):
        angle = w * (m % LANES)
        return np.cos(angle) + np.sin(angle)

    first, second = np.outer(q, q), np.outer(q, q + 1)
    table = np.block([[cas(first), cas(second)], [-cas(-first), cas(-second)]])

    def parts(array):
        array = array.astype(np.float32)
        high = array.astype(ml_dtypes.bfloat16)
        low = (array - high.astype(np.float32)).astype(ml_dtypes.bfloat16)
        return np.stack([high, low])

    psi = 2.0 * np.pi * np.outer(np.arange(9), q) / NP
    twiddle = np.stack([np.cos(psi), np.sin(psi)]).astype(np.float32)
    return parts(table), parts(table.T / NP), twiddle[:, :, None, :]


def cosine(m):
    return math.cos(2.0 * math.pi * (m % 16) / 16)


def sine(m):
    return math.sin(2.0 * math.pi * (m % 16) / 16)


def weighted(terms):
    total = None
    for weight, value in terms:
        if abs(weight) < 1e-9:
            continue
        if abs(weight - 1.0) < 1e-9:
            total = value if total is None else total + value
        elif abs(weight + 1.0) < 1e-9:
            total = -value if total is None else total - value
        else:
            total = weight * value if total is None else total + weight * value
    return total


def forward_16(x):
    e = [None] + [x[p] + x[16 - p] for p in range(1, 8)]
    o = [None] + [x[p] - x[16 - p] for p in range(1, 8)]
    x_even, x_odd = x[0] + x[8], x[0] - x[8]
    ee = [None] + [e[p] + e[8 - p] for p in range(1, 4)]
    eo = [None] + [e[p] - e[8 - p] for p in range(1, 4)]
    oo = [None] + [o[p] + o[8 - p] for p in range(1, 4)]
    oe = [None] + [o[p] - o[8 - p] for p in range(1, 4)]
    cs, ss = [], []
    for c in range(9):
        if c % 2 == 0:
            cs.append(weighted([(1.0, x_even), (cosine(4 * c), e[4])] + [(cosine(p * c), ee[p]) for p in range(1, 4)]))
            ss.append(weighted([(sine(p * c), oe[p]) for p in range(1, 4)]) if 0 < c < 8 else None)
        else:
            cs.append(weighted([(1.0, x_odd)] + [(cosine(p * c), eo[p]) for p in range(1, 4)]))
            ss.append(weighted([(sine(4 * c), o[4])] + [(sine(p * c), oo[p]) for p in range(1, 4)]))
    return cs, ss


def inverse_16(cs, ss):
    x = [None] * 16
    x[0] = weighted([(1.0, v) for v in cs])
    x[8] = weighted([((-1.0) ** c, v) for c, v in enumerate(cs)])
    for p in range(1, 5):
        ev = weighted([(1.0, cs[0]), (cosine(8 * p), cs[8])] + [(cosine(p * c), cs[c]) for c in range(2, 8, 2)])
        eo = weighted([(cosine(p * c), cs[c]) for c in range(1, 8, 2)])
        ov = weighted([(sine(p * c), ss[c]) for c in range(2, 8, 2)])
        oo = weighted([(sine(p * c), ss[c]) for c in range(1, 8, 2)])
        if p == 4:
            x[4], x[12] = ev + oo, ev - oo
            continue
        x[p] = (ev + eo) + (ov + oo)
        x[16 - p] = (ev + eo) - (ov + oo)
        x[8 - p] = (ev - eo) + (oo - ov)
        x[8 + p] = (ev - eo) - (oo - ov)
    return x


def split_dot(values, table_ref):
    high = values.astype(bf16)
    low = (values - high.astype(f32)).astype(bf16)

    def dot(left, right):
        return jnp.dot(left, right, preferred_element_type=f32)

    return dot(high, table_ref[0]) + dot(low, table_ref[0]) + dot(high, table_ref[1])


def section_kernel(
    off_ref, st_ref, ro_ref, blend_hbm, jac_hbm, mix_hbm, table_hbm, back_hbm, twiddle_hbm, band_hbm,
    partial, ghost_ref, weights, mixes,
    cells, planes, spectrum, blends, turned, outgoing, pitch_pack, pitch_recv, span_pack, span_recv,
    bent_a, bent_b, rows_a, rows_b, radial, kept, edge_fix, permuted, blend_v, jac_v, mix_v, table_ref, back_ref, twiddle_ref, band_ref,
    load_sem, own_sem, row_send, row_recv, back_send, back_recv, halo_send, halo_recv, small_sem,
):
    me = lax.axis_index("pitch")
    span = lax.axis_index("span")
    left, right = lax.rem(me + 15, 16), lax.rem(me + 1, 16)
    targets = [4 * lax.rem(me // 4 + dx, 4) + lax.rem(me + dz, 4) for dx, dz in ORDER]
    below, above = lax.rem(span + 7, 8), lax.rem(span + 1, 8)
    states = (st_ref, ro_ref)

    def load(s, f):
        return pltpu.make_async_copy(states[s].at[f], cells.at[s, f, pl.ds(2, AX), pl.ds(8, ROWS)], load_sem.at[s, f])

    def row_block(s, target, first=0, count=FIELDS):
        layer, block = target // 8, target % 8
        axial = 15 - layer if s == 0 else layer
        rows = pl.ds(pl.multiple_of(8 * block, 8), 8)
        return states[s].at[pl.ds(first, count), axial, rows, :]

    def own_rows(s):
        return pltpu.make_async_copy(row_block(s, me), planes.at[s, me], own_sem.at[s])

    barrier = pltpu.get_barrier_semaphore()

    def greet(j, carry):
        pl.semaphore_signal(barrier, inc=1, device_id={"pitch": lax.rem(me + j, 16)}, device_id_type=MESH)
        return carry

    lax.fori_loop(1, 16, greet, 0)
    for other in (below, above):
        pl.semaphore_signal(barrier, inc=1, device_id={"span": other}, device_id_type=MESH)

    smalls = [
        pltpu.make_async_copy(source, target, small_sem.at[i])
        for i, (source, target) in enumerate((
            (blend_hbm, blend_v), (jac_hbm, jac_v), (mix_hbm, mix_v),
            (table_hbm, table_ref), (back_hbm, back_ref), (twiddle_hbm, twiddle_ref), (band_hbm, band_ref),
        ))
    ]
    for s in range(2):
        own_rows(s).start()
    for s in range(2):
        for f in range(FIELDS):
            load(s, f).start()
    for copy in smalls:
        copy.start()

    lane = lax.broadcasted_iota(jnp.int32, (8, LANES), 1)
    row = lax.broadcasted_iota(jnp.int32, (8, LANES), 0)
    group = lane % 4
    nothing = jnp.zeros((8, LANES), f32)
    scale = time_step * damping
    for s in range(2):
        for f in range(FIELDS):
            for t in range(8):
                for a in (0, 1, 18, 19):
                    cells[s, f, a, 8 + 8 * t:16 + 8 * t, :] = nothing

    for copy in smalls:
        copy.wait()
    for d in range(3):
        for f in range(FIELDS):
            for g in range(FIELDS):
                value = jnp.broadcast_to(jac_v[f, d:d + 1, g:g + 1], (8, LANES))
                weights[(d * FIELDS + g) * FIELDS + f] = (-0.5 * time_step) * value
    for f in range(FIELDS):
        for g in range(FIELDS):
            mixes[f * FIELDS + g] = jnp.broadcast_to(mix_v[f:f + 1, g:g + 1], (8, LANES))

    spot = lax.broadcasted_iota(jnp.int32, (24, 256), 1)
    field = sum((spot >= 48 * g).astype(jnp.int32) for g in range(1, FIELDS + 1))
    place = spot - 48 * field
    for block in range(2):
        step = place - lax.broadcasted_iota(jnp.int32, (24, 256), 0) - (8 + 8 * block)
        side = (step == 1).astype(f32) - (step == -1).astype(f32)
        blur = (4.0 * scale) * (jnp.abs(step) == 1).astype(f32) - scale * (jnp.abs(step) == 2).astype(f32)
        for f in range(FIELDS):
            value = jnp.where(field == f, blur, 0.0)
            for g in range(FIELDS):
                weight = jnp.broadcast_to(weights[(FIELDS + g) * FIELDS + f][0:1, 0:1], (24, 256))
                value = value + jnp.where(field == g, weight * side, 0.0)
            high = value.astype(bf16).astype(f32)
            low = value - high
            radial[block, f] = jnp.concatenate([high, low, high], axis=1)

    spare = jnp.zeros((3, LANES), f32)
    blend_rows = jnp.concatenate(
        [part for t in range(TILES) for part in (blend_v[:, LANES * t:LANES * t + LANES], spare)], axis=0
    )
    source_lane = lax.broadcasted_iota(jnp.int32, (LANES, LANES), 0)
    target_lane = lax.broadcasted_iota(jnp.int32, (LANES, LANES), 1)
    chosen = (8 * (source_lane % 16) + source_lane // 16 == target_lane).astype(f32)
    permuted[...] = jnp.dot(
        blend_rows, chosen, precision=lax.Precision.HIGHEST, preferred_element_type=f32
    ).reshape(TILES, 8, LANES)

    def mode_row(k):
        total = nothing
        for t in range(TILES):
            shift = (8 * (t - k)) % LANES
            value = permuted[t]
            total = jnp.where(lane // 8 == t, pltpu.roll(value, shift, 1) if shift else value, total)
        return total

    for c in range(9):
        near = mode_row(c)
        other = mode_row(16 - c) if 0 < c < 8 else nothing
        for f in range(FIELDS):
            blends[c, f, :, 0:LANES] = jnp.broadcast_to(near[f:f + 1, :], (8, LANES))
            blends[c, f, :, LANES:] = jnp.broadcast_to(other[f:f + 1, :], (8, LANES))

    pl.semaphore_wait(barrier, 17)

    def row_copy(s, chunk, target, source):
        first, count = CHUNKS[chunk]
        return pltpu.make_async_remote_copy(
            src_ref=row_block(s, target, first, count), dst_ref=planes.at[s, source, pl.ds(first, count)],
            send_sem=row_send.at[s, chunk, target], recv_sem=row_recv.at[s, chunk, source],
            device_id={"pitch": target}, device_id_type=MESH,
        )

    for chunk in range(len(CHUNKS)):

        for target in targets:
            for s in range(2):
                row_copy(s, chunk, target, me).start()

    def halo_copy(slot, src, dst, where):
        return pltpu.make_async_remote_copy(
            src_ref=src, dst_ref=dst, send_sem=halo_send.at[slot], recv_sem=halo_recv.at[slot],
            device_id=where, device_id_type=MESH,
        )

    to_above = halo_copy(0, span_pack.at[0], span_recv.at[0], {"span": above})
    to_below = halo_copy(1, span_pack.at[1], span_recv.at[1], {"span": below})
    to_right = halo_copy(2, pitch_pack.at[0], pitch_recv.at[0], {"pitch": right})
    to_left = halo_copy(3, pitch_pack.at[1], pitch_recv.at[1], {"pitch": left})

    for s in range(2):
        for f in range(FIELDS):
            load(s, f).wait()

        def pack(pair, carry):
            found = []
            for half in range(2):
                m = 2 * pair + half
                f, first = m // 4, 2 + 4 * (m % 4)
                edge = jnp.zeros((8, LANES), f32)
                low = jnp.zeros((8, LANES), f32)
                high = jnp.zeros((8, LANES), f32)
                for j in range(4):
                    for t in range(8):
                        n = 8 * j + t
                        value = cells[s, f, first + j, 8 + 8 * t:16 + 8 * t, :]
                        edge = jnp.where(lane // 4 == n, pltpu.roll(value, (2 + 4 * n) % LANES, 1), edge)
                        if t == 0:
                            low = jnp.where(row // 2 == j, pltpu.roll(value, 2 * j, 0) if j else value, low)
                        if t == 7:
                            shift = (2 * j + 2) % 8
                            high = jnp.where(row // 2 == j, pltpu.roll(value, shift, 0) if shift else value, high)
                span_pack[0, s, m] = high
                span_pack[1, s, m] = low
                found.append(edge)
            pitch_pack[0, s, pair] = jnp.where(group < 2, found[0], pltpu.roll(found[1], 2, 1))
            pitch_pack[1, s, pair] = jnp.where(group < 2, pltpu.roll(found[0], LANES - 2, 1), found[1])
            return carry

        lax.fori_loop(0, 10, pack, 0)
    for copy in (to_above, to_below, to_right, to_left):
        copy.start()

    def base_ghosts(block, carry):
        rows = pl.ds(pl.multiple_of(8 + 8 * block, 8), 8)
        for s in range(2):
            for layer in range(2):
                kept = [cells[s, g, 17 - layer if s == 0 else 2 + layer, rows, :] for g in range(FIELDS)]
                for f in range(FIELDS):
                    total = mixes[f * FIELDS] * kept[0]
                    for g in range(1, FIELDS):
                        total = total + mixes[f * FIELDS + g] * kept[g]
                    cells[s, f, 18 + layer if s == 0 else 1 - layer, rows, :] = total
        return carry

    lax.fori_loop(0, 8, base_ghosts, 0)

    rim = (lane < 2) | (lane >= LANES - 2)

    def products(layer, bent, rows_out):
        highs, lows = [], []
        for k in range(2):
            s, a = (layer + k) // AX, (layer + k) % AX
            values = cells[s, :, a + 2, 8:8 + ROWS, :].reshape(FIELDS * ROWS, LANES)
            high = values.astype(bf16)
            low = (values - high.astype(f32)).astype(bf16)
            both = jnp.concatenate([high, low], axis=1)
            bent[k] = jnp.dot(both, band_ref[...], preferred_element_type=f32).reshape(FIELDS, ROWS, 256)
            highs.append(high)
            lows.append(low)
        blank = jnp.zeros((16, LANES), bf16)
        for block in range(2):

            def stacked(parts):
                return jnp.concatenate([
                    jnp.concatenate(
                        [part[ROWS * g + 16 * block:ROWS * g + 16 * block + 48, :] for g in range(FIELDS)] + [blank], axis=0
                    )
                    for part in parts
                ], axis=1)

            upper = stacked(highs)
            data = jnp.concatenate([upper, upper, stacked(lows)], axis=0)
            left = radial[block].reshape(FIELDS * 24, 768).astype(bf16)
            rows_out[block] = jnp.dot(left, data, preferred_element_type=f32).reshape(FIELDS, 24, 256)

    def pitch_fix(s, f, a, tile):
        amount = lax.rem(126 - 32 * lax.rem(a, 4) - 4 * tile + 2 * LANES, LANES)
        return jnp.where(rim, pltpu.roll(edge_fix[s, f, a // 4], amount, 1), 0.0)

    def sweep(layer, first, rows, bent, fixed):
        s, a = layer // AX, layer % AX
        count = rows // 8
        sums = [None] * FIELDS
        for g in range(FIELDS):

            def get(axial, radial):
                start = 8 + first + radial
                return cells[s, g, a + 2 + axial, start:start + rows, :].reshape(count, 8, LANES)

            ahead, behind = get(1, 0), get(-1, 0)
            up, down = get(0, 1), get(0, -1)
            near = (ahead + behind) + (up + down)
            far = (get(2, 0) + get(-2, 0)) + (get(0, 2) + get(0, -2))
            own = bent(g)[:, LANES:].reshape(count, 8, LANES) + ((4.0 * scale) * near - scale * far)
            along = bent(g)[:, 0:LANES].reshape(count, 8, LANES)
            if fixed:
                own = own + jnp.stack([pitch_fix(s, g, a, first // 8 + t) for t in range(count)])
            sums[g] = own if sums[g] is None else sums[g] + own
            for d, slope in enumerate((ahead - behind, up - down, along)):
                for f in range(FIELDS):
                    term = weights[(d * FIELDS + g) * FIELDS + f] * slope
                    sums[f] = term if sums[f] is None else sums[f] + term
        for f in range(FIELDS):
            partial[s, f, a, first:first + rows, :] = sums[f].reshape(rows, LANES)

    def inner(layer, k, bent, rows_in, fixed):
        s, a = layer // AX, layer % AX
        sums = [
            jnp.concatenate([rows_in[block, f, :, LANES * k:LANES * k + LANES] for block in range(2)], axis=0).reshape(6, 8, LANES)
            for f in range(FIELDS)
        ]
        for g in range(FIELDS):

            def get(axial):
                return cells[s, g, a + 2 + axial, 16:8 + ROWS - 8, :].reshape(6, 8, LANES)

            ahead, behind = get(1), get(-1)
            along = bent[k, g, 8:ROWS - 8, 0:LANES].reshape(6, 8, LANES)
            own = bent[k, g, 8:ROWS - 8, LANES:].reshape(6, 8, LANES)
            own = own + ((4.0 * scale) * (ahead + behind) - scale * (get(2) + get(-2)))
            if fixed:
                own = own + jnp.stack([pitch_fix(s, g, a, 1 + t) for t in range(6)])
            sums[g] = sums[g] + own
            for d, slope in ((0, ahead - behind), (2, along)):
                for f in range(FIELDS):
                    sums[f] = sums[f] + weights[(d * FIELDS + g) * FIELDS + f] * slope
        for f in range(FIELDS):
            partial[s, f, a, 8:ROWS - 8, :] = sums[f].reshape(48, LANES)

    def early_layer(layer, k, bent, rows_in):
        inner(layer, k, bent, rows_in, False)
        kept[layer, :, 0:8, :] = bent[k, :, 0:8, :]
        kept[layer, :, 8:16, :] = bent[k, :, ROWS - 8:, :]

    def late_layer(layer, k, bent, rows_in):
        inner(layer, k, bent, rows_in, True)
        sweep(layer, 0, 8, lambda g: bent[k, g, 0:8, :], True)
        sweep(layer, ROWS - 8, 8, lambda g: bent[k, g, ROWS - 8:, :], True)

    def finish_early(layer, carry):
        s, a = layer // AX, layer % AX
        sweep(layer, 0, 8, lambda g: kept[layer, g, 0:8, :], True)
        sweep(layer, ROWS - 8, 8, lambda g: kept[layer, g, 8:16, :], True)
        for f in range(FIELDS):
            for t in range(1, 7):
                partial[s, f, a, 8 * t:8 * t + 8, :] = partial[s, f, a, 8 * t:8 * t + 8, :] + pitch_fix(s, f, a, t)
        return carry

    def layers(first, last, step):
        products(first, bent_a, rows_a)

        def four_layers(i, carry):
            products(4 * i + 2, bent_b, rows_b)
            step(4 * i, 0, bent_a, rows_a)
            step(4 * i + 1, 1, bent_a, rows_a)
            products(jnp.minimum(4 * i + 4, last - 2), bent_a, rows_a)
            step(4 * i + 2, 0, bent_b, rows_b)
            step(4 * i + 3, 1, bent_b, rows_b)
            return carry

        lax.fori_loop(first // 4, last // 4, four_layers, 0)


    offset = off_ref[0]
    shift, hop = lax.rem(offset, LANES), offset // LANES

    for s in range(2):
        own_rows(s).wait()

    def back_copy(chunk, target, source):
        first, count = CHUNKS[chunk]
        return pltpu.make_async_remote_copy(
            src_ref=outgoing.at[target, :, pl.ds(first, count)], dst_ref=ghost_ref.at[source, :, pl.ds(first, count)],
            send_sem=back_send.at[chunk, target], recv_sem=back_recv.at[chunk, source],
            device_id={"pitch": target}, device_id_type=MESH,
        )

    for chunk, (start, count) in enumerate(CHUNKS):
        done = sum(BEFORE[:chunk])
        if BEFORE[chunk]:
            layers(done, done + BEFORE[chunk], early_layer)

        def wait_rows(j, carry):
            source = lax.rem(me + j, 16)
            for s in range(2):
                row_copy(s, chunk, source, source).wait_recv()
            return carry

        lax.fori_loop(1, 16, wait_rows, 0)

        def forward(f, carry):
            for t in range(TILES):
                turned[t] = pltpu.roll(planes[1, t, f], shift, 1)
            x = []
            for t in range(TILES):
                near = turned[lax.rem(t + 16 - hop, 16)]
                far = turned[lax.rem(t + 15 - hop, 16)]
                x.append(jnp.where(lane >= shift, near, far) - planes[0, t, f])
            cs, ss = forward_16(x)
            for c in range(9):
                cosines, sines = twiddle_ref[0, c], twiddle_ref[1, c]
                if c == 0:
                    real, imaginary = cs[0], nothing
                elif c == 8:
                    real, imaginary = cs[8] * cosines, -(cs[8] * sines)
                else:
                    real = cs[c] * cosines - ss[c] * sines
                    imaginary = -(cs[c] * sines + ss[c] * cosines)
                spectrum[c, f, :, 0:LANES] = real
                spectrum[c, f, :, LANES:] = imaginary
            return carry

        lax.fori_loop(start, start + count, forward, 0)
        modes = split_dot(spectrum[:, start:start + count].reshape(72 * count, 256), table_ref)
        modes = modes * blends[:, start:start + count].reshape(72 * count, 256)
        spectrum[:, start:start + count] = split_dot(modes, back_ref).reshape(9, count, 8, 256)

        def inverse(f, carry):
            cs, ss = [], []
            for c in range(9):
                cosines, sines = twiddle_ref[0, c], twiddle_ref[1, c]
                real, imaginary = spectrum[c, f, :, 0:LANES], spectrum[c, f, :, LANES:]
                cs.append(real * cosines - imaginary * sines)
                ss.append(-(real * sines + imaginary * cosines))
            x = inverse_16(cs, ss)
            for t in range(TILES):
                outgoing[t, 0, f] = x[t]
                turned[t] = pltpu.roll(x[t], lax.rem(LANES - shift, LANES), 1)
            for t in range(TILES):
                near = turned[lax.rem(t + hop, 16)]
                far = turned[lax.rem(t + hop + 1, 16)]
                outgoing[t, 1, f] = jnp.where(lane < LANES - shift, near, far)
            return carry

        lax.fori_loop(start, start + count, inverse, 0)

        for target in targets:
            back_copy(chunk, target, me).start()

    own_back = pltpu.make_async_copy(outgoing.at[me], ghost_ref.at[me], own_sem.at[0])
    own_back.start()

    for copy in (to_above, to_below, to_right, to_left):
        copy.wait()
    keep_low = jnp.where(span == 0, 0.0, 1.0).astype(f32)
    keep_high = jnp.where(span == 7, 0.0, 1.0).astype(f32)
    for s in range(2):

        def unpack(m, carry):
            f, first = m // 4, 4 * (m % 4)
            low = span_recv[0, s, m] * keep_low
            high = span_recv[1, s, m] * keep_high
            for j in range(4):
                cells[s, f, 2 + first + j, 6:8, :] = low[2 * j:2 * j + 2, :]
                cells[s, f, 2 + first + j, 72:74, :] = high[2 * j:2 * j + 2, :]
            return carry

        lax.fori_loop(0, 20, unpack, 0)

        def edges(quarter_pair, carry):
            total = [[None] * FIELDS, [None] * FIELDS]
            for g in range(FIELDS):
                from_left, from_right = pitch_recv[0, s, 2 * g + quarter_pair], pitch_recv[1, s, 2 * g + quarter_pair]
                for half in range(2):
                    if half == 0:
                        halo = jnp.where(group < 2, from_left, pltpu.roll(from_right, 2, 1))
                    else:
                        halo = jnp.where(group < 2, pltpu.roll(from_left, LANES - 2, 1), from_right)
                    plus_1, minus_1 = pltpu.roll(halo, LANES - 1, 1), pltpu.roll(halo, 1, 1)
                    plus_2, minus_2 = pltpu.roll(halo, LANES - 2, 1), pltpu.roll(halo, 2, 1)
                    slope = jnp.where(group == 1, plus_1, jnp.where(group == 2, -minus_1, 0.0))
                    smooth = jnp.where(group < 2, plus_2, minus_2) - 4.0 * jnp.where(
                        group == 1, plus_1, jnp.where(group == 2, minus_1, 0.0)
                    )
                    for f in range(FIELDS):
                        term = weights[(2 * FIELDS + g) * FIELDS + f] * slope
                        if f == g:
                            term = term - scale * smooth
                        total[half][f] = term if total[half][f] is None else total[half][f] + term
            for half in range(2):
                for f in range(FIELDS):
                    edge_fix[s, f, 2 * quarter_pair + half] = total[half][f]
            return carry

        lax.fori_loop(0, 2, edges, 0)

    layers(EARLY, 2 * AX, late_layer)
    lax.fori_loop(0, EARLY, finish_early, 0)

    own_back.wait()

    def finish(j, carry):
        other = lax.rem(me + j, 16)
        for chunk in range(len(CHUNKS)):
            for s in range(2):
                row_copy(s, chunk, other, me).wait_send()
            back_copy(chunk, other, me).wait_send()
            back_copy(chunk, other, other).wait_recv()
        return carry

    lax.fori_loop(1, 16, finish, 0)


def band_table():
    position = np.arange(LANES)
    scale = time_step * damping
    slope = np.zeros((LANES, LANES))
    smooth = np.zeros((LANES, LANES))
    for step, weight in ((1, 1.0), (-1, -1.0)):
        inside = position[(position + step >= 0) & (position + step < LANES)]
        slope[inside + step, inside] += weight
    for step, weight in ((0, 1.0 - 18.0 * scale), (1, 4.0 * scale), (-1, 4.0 * scale), (2, -scale), (-2, -scale)):
        inside = position[(position + step >= 0) & (position + step < LANES)]
        smooth[inside + step, inside] += weight
    table = np.concatenate([slope, smooth], axis=1)
    return np.concatenate([table, table], axis=0).astype(ml_dtypes.bfloat16)


def section(offset, stator, rotor, blend, jacobians, field_mix):
    forward_table, back_table, twiddle = transform_tables()
    whole = pl.BlockSpec(memory_space=pltpu.VMEM)
    anywhere = pl.BlockSpec(memory_space=pl.ANY)
    dma = pltpu.SemaphoreType.DMA
    return pl.pallas_call(
        section_kernel,
        name="section",
        out_shape=(
            pltpu.VMEM((2, FIELDS, AX, ROWS, LANES), f32),
            pltpu.VMEM((16, 2, FIELDS, 8, LANES), f32),
            pltpu.VMEM((75, 8, LANES), f32),
            pltpu.VMEM((25, 8, LANES), f32),
        ),
        in_specs=[pl.BlockSpec(memory_space=pltpu.SMEM)] + [pl.BlockSpec(memory_space=pltpu.HBM)] * 9,
        out_specs=(whole, whole, whole, whole),
        scratch_shapes=[
            pltpu.VMEM((2, FIELDS, AX + 4, ROWS + 16, LANES), f32),
            pltpu.VMEM((2, 16, FIELDS, 8, LANES), f32),
            pltpu.VMEM((9, FIELDS, 8, 256), f32),
            pltpu.VMEM((9, FIELDS, 8, 256), f32),
            pltpu.VMEM((16, 8, LANES), f32),
            pltpu.VMEM((16, 2, FIELDS, 8, LANES), f32),
            pltpu.VMEM((2, 2, 10, 8, LANES), f32),
            pltpu.VMEM((2, 2, 10, 8, LANES), f32),
            pltpu.VMEM((2, 2, 20, 8, LANES), f32),
            pltpu.VMEM((2, 2, 20, 8, LANES), f32),
            pltpu.VMEM((2, FIELDS, ROWS, 256), f32),
            pltpu.VMEM((2, FIELDS, ROWS, 256), f32),
            pltpu.VMEM((2, FIELDS, 24, 256), f32),
            pltpu.VMEM((2, FIELDS, 24, 256), f32),
            pltpu.VMEM((2, FIELDS, 24, 768), f32),
            pltpu.VMEM((EARLY, FIELDS, 16, 256), f32),
            pltpu.VMEM((2, FIELDS, 4, 8, LANES), f32),
            pltpu.VMEM((TILES, 8, LANES), f32),
            pltpu.VMEM((FIELDS, NP), f32),
            pltpu.VMEM((FIELDS, 3, FIELDS), f32),
            pltpu.VMEM((FIELDS, FIELDS), f32),
            pltpu.VMEM((2, 256, 256), bf16),
            pltpu.VMEM((2, 256, 256), bf16),
            pltpu.VMEM((2, 9, 1, LANES), f32),
            pltpu.VMEM((256, 256), bf16),
            dma((2, FIELDS)), dma((2,)), dma((2, len(CHUNKS), 16)), dma((2, len(CHUNKS), 16)), dma((len(CHUNKS), 16)), dma((len(CHUNKS), 16)),
            dma((4,)), dma((4,)), dma((7,)),
        ],
        compiler_params=pltpu.CompilerParams(
            collective_id=0, has_side_effects=True, vmem_limit_bytes=32 << 20
        ),
    )(offset, *(
        pltpu.with_memory_space_constraint(jnp.asarray(x), pltpu.HBM)
        for x in (
            stator, rotor, blend, jacobians.transpose(1, 0, 2), field_mix,
            forward_table, back_table, twiddle, band_table(),
        )
    ))


def close_kernel(partial, ghosts, weights, mixes, st_out, ro_out, ends, store_sem, end_sem):
    outs = (st_out, ro_out)
    scale = time_step * damping
    copies = []
    for s in range(2):
        first = 0 if s == 0 else 2
        for f in range(FIELDS):
            copies.append(pltpu.make_async_copy(
                partial.at[s, f, pl.ds(first, AX - 2)], outs[s].at[f, pl.ds(first, AX - 2)], store_sem.at[s, f]
            ))
    for copy in copies:
        copy.start()

    for s in range(2):

        def fill(block, carry):
            rows = pl.ds(pl.multiple_of(8 * block, 8), 8)
            mixed = []
            for layer in range(2):
                parts = [ghosts[8 * layer + block, s, g] for g in range(FIELDS)]
                found = []
                for f in range(FIELDS):
                    total = mixes[f * FIELDS] * parts[0]
                    for g in range(1, FIELDS):
                        total = total + mixes[f * FIELDS + g] * parts[g]
                    found.append(total if s == 0 else -total)
                mixed.append(found)
            outer, inner = (15, 14) if s == 0 else (0, 1)
            for f in range(FIELDS):
                total = (4.0 * scale) * mixed[0][f] - scale * mixed[1][f]
                for g in range(FIELDS):
                    term = weights[g * FIELDS + f] * mixed[0][g]
                    total = total + term if s == 0 else total - term
                ends[s, f, outer % 2, rows, :] = partial[s, f, outer, rows, :] + total
                ends[s, f, inner % 2, rows, :] = partial[s, f, inner, rows, :] - scale * mixed[0][f]
            return carry

        lax.fori_loop(0, 8, fill, 0)
        last = pltpu.make_async_copy(ends.at[s], outs[s].at[:, pl.ds(14 if s == 0 else 0, 2)], end_sem.at[s])
        last.start()
        copies.append(last)
    for copy in copies:
        copy.wait()


def close(partial, ghosts, weights, mixes):
    anywhere = pl.BlockSpec(memory_space=pl.ANY)
    whole = pl.BlockSpec(memory_space=pltpu.VMEM)
    dma = pltpu.SemaphoreType.DMA
    shape = jax.ShapeDtypeStruct((FIELDS, AX, ROWS, LANES), f32)
    return pl.pallas_call(
        close_kernel,
        name="close",
        out_shape=(shape, shape),
        in_specs=[whole] * 4,
        out_specs=(anywhere, anywhere),
        scratch_shapes=[pltpu.VMEM((2, FIELDS, 2, ROWS, LANES), f32), dma((2, FIELDS)), dma((2,))],
        compiler_params=pltpu.CompilerParams(vmem_limit_bytes=8 << 20),
    )(partial, ghosts, weights, mixes)


def shards(stator_state, rotor_state, jacobians, field_mix, mode_blend, rotor_offset):
    parts = section(rotor_offset, stator_state, rotor_state, mode_blend, jacobians, field_mix)
    return close(*parts)


def solution(mesh):
    in_specs = (P(None, None, "span", "pitch"), P(None, None, "span", "pitch"), P(), P(), P(), P())
    out_specs = (P(None, None, "span", "pitch"), P(None, None, "span", "pitch"))
    return jax.shard_map(shards, mesh=mesh, in_specs=in_specs, out_specs=out_specs, check_vma=False)
```

```python
import math

import jax
import jax.numpy as jnp
import ml_dtypes
import numpy as np
from jax import lax
from jax.experimental import pallas as pl
from jax.experimental.pallas import tpu as pltpu
from jax.sharding import PartitionSpec as P

NP = 2048
FIELDS = 5
AX = 16
ROWS = 64
LANES = 128
TILES = 16
MESH = pl.DeviceIdType.MESH
EARLY = 12
BEFORE = (12,)
CHUNKS = ((0, 5),)
ORDER = (
    (2, 2), (2, 3), (3, 2), (2, 1), (1, 2), (2, 0), (0, 2), (3, 1), (1, 3), (3, 3), (1, 1), (3, 0), (0, 3), (1, 0), (0, 1),
)
f32 = jnp.float32
bf16 = jnp.bfloat16

time_step = 0.5
damping = 1.0 / 32.0


def transform_tables():
    q = np.arange(LANES)
    w = 2.0 * np.pi / LANES

    def cas(m):
        angle = w * (m % LANES)
        return np.cos(angle) + np.sin(angle)

    first, second = np.outer(q, q), np.outer(q, q + 1)
    table = np.block([[cas(first), cas(second)], [-cas(-first), cas(-second)]])

    def parts(array):
        array = array.astype(np.float32)
        high = array.astype(ml_dtypes.bfloat16)
        low = (array - high.astype(np.float32)).astype(ml_dtypes.bfloat16)
        return np.stack([high, low])

    psi = 2.0 * np.pi * np.outer(np.arange(9), q) / NP
    twiddle = np.stack([np.cos(psi), np.sin(psi)]).astype(np.float32)
    return parts(table), parts(table.T / NP), twiddle[:, :, None, :]


def cosine(m):
    return math.cos(2.0 * math.pi * (m % 16) / 16)


def sine(m):
    return math.sin(2.0 * math.pi * (m % 16) / 16)


def weighted(terms):
    total = None
    for weight, value in terms:
        if abs(weight) < 1e-9:
            continue
        if abs(weight - 1.0) < 1e-9:
            total = value if total is None else total + value
        elif abs(weight + 1.0) < 1e-9:
            total = -value if total is None else total - value
        else:
            total = weight * value if total is None else total + weight * value
    return total


def forward_16(x):
    e = [None] + [x[p] + x[16 - p] for p in range(1, 8)]
    o = [None] + [x[p] - x[16 - p] for p in range(1, 8)]
    x_even, x_odd = x[0] + x[8], x[0] - x[8]
    ee = [None] + [e[p] + e[8 - p] for p in range(1, 4)]
    eo = [None] + [e[p] - e[8 - p] for p in range(1, 4)]
    oo = [None] + [o[p] + o[8 - p] for p in range(1, 4)]
    oe = [None] + [o[p] - o[8 - p] for p in range(1, 4)]
    cs, ss = [], []
    for c in range(9):
        if c % 2 == 0:
            cs.append(weighted([(1.0, x_even), (cosine(4 * c), e[4])] + [(cosine(p * c), ee[p]) for p in range(1, 4)]))
            ss.append(weighted([(sine(p * c), oe[p]) for p in range(1, 4)]) if 0 < c < 8 else None)
        else:
            cs.append(weighted([(1.0, x_odd)] + [(cosine(p * c), eo[p]) for p in range(1, 4)]))
            ss.append(weighted([(sine(4 * c), o[4])] + [(sine(p * c), oo[p]) for p in range(1, 4)]))
    return cs, ss


def inverse_16(cs, ss):
    x = [None] * 16
    x[0] = weighted([(1.0, v) for v in cs])
    x[8] = weighted([((-1.0) ** c, v) for c, v in enumerate(cs)])
    for p in range(1, 5):
        ev = weighted([(1.0, cs[0]), (cosine(8 * p), cs[8])] + [(cosine(p * c), cs[c]) for c in range(2, 8, 2)])
        eo = weighted([(cosine(p * c), cs[c]) for c in range(1, 8, 2)])
        ov = weighted([(sine(p * c), ss[c]) for c in range(2, 8, 2)])
        oo = weighted([(sine(p * c), ss[c]) for c in range(1, 8, 2)])
        if p == 4:
            x[4], x[12] = ev + oo, ev - oo
            continue
        x[p] = (ev + eo) + (ov + oo)
        x[16 - p] = (ev + eo) - (ov + oo)
        x[8 - p] = (ev - eo) + (oo - ov)
        x[8 + p] = (ev - eo) - (oo - ov)
    return x


def split_dot(values, table_ref):
    high = values.astype(bf16)
    low = (values - high.astype(f32)).astype(bf16)

    def dot(left, right):
        return jnp.dot(left, right, preferred_element_type=f32)

    return dot(high, table_ref[0]) + dot(low, table_ref[0]) + dot(high, table_ref[1])


def section_kernel(
    off_ref, st_ref, ro_ref, blend_hbm, jac_hbm, mix_hbm, table_hbm, back_hbm, twiddle_hbm, band_hbm,
    partial, ghost_ref, weights, mixes,
    cells, planes, spectrum, blends, turned, outgoing, pitch_pack, pitch_recv, span_pack, span_recv,
    bent_a, bent_b, rows_a, rows_b, radial, kept, edge_fix, permuted, blend_v, jac_v, mix_v, table_ref, back_ref, twiddle_ref, band_ref,
    load_sem, own_sem, row_send, row_recv, back_send, back_recv, halo_send, halo_recv, small_sem,
):
    me = lax.axis_index("pitch")
    span = lax.axis_index("span")
    left, right = lax.rem(me + 15, 16), lax.rem(me + 1, 16)
    targets = [4 * lax.rem(me // 4 + dx, 4) + lax.rem(me + dz, 4) for dx, dz in ORDER]
    sources = [4 * lax.rem(me // 4 + 4 - dx, 4) + lax.rem(me + 4 - dz, 4) for dx, dz in ORDER]
    below, above = lax.rem(span + 7, 8), lax.rem(span + 1, 8)
    states = (st_ref, ro_ref)

    def load(s, f):
        return pltpu.make_async_copy(states[s].at[f], cells.at[s, f, pl.ds(2, AX), pl.ds(8, ROWS)], load_sem.at[s, f])

    def row_block(s, target, first=0, count=FIELDS):
        layer, block = target // 8, target % 8
        axial = 15 - layer if s == 0 else layer
        rows = pl.ds(pl.multiple_of(8 * block, 8), 8)
        return states[s].at[pl.ds(first, count), axial, rows, :]

    def own_rows(s):
        return pltpu.make_async_copy(row_block(s, me), planes.at[s, me], own_sem.at[s])

    barrier = pltpu.get_barrier_semaphore()

    def greet(j, carry):
        pl.semaphore_signal(barrier, inc=1, device_id={"pitch": lax.rem(me + j, 16)}, device_id_type=MESH)
        return carry

    lax.fori_loop(1, 16, greet, 0)
    for other in (below, above):
        pl.semaphore_signal(barrier, inc=1, device_id={"span": other}, device_id_type=MESH)

    smalls = [
        pltpu.make_async_copy(source, target, small_sem.at[i])
        for i, (source, target) in enumerate((
            (blend_hbm, blend_v), (jac_hbm, jac_v), (mix_hbm, mix_v),
            (table_hbm, table_ref), (back_hbm, back_ref), (twiddle_hbm, twiddle_ref), (band_hbm, band_ref),
        ))
    ]
    for s in range(2):
        own_rows(s).start()
    for s in range(2):
        for f in range(FIELDS):
            load(s, f).start()
    for copy in smalls:
        copy.start()

    lane = lax.broadcasted_iota(jnp.int32, (8, LANES), 1)
    row = lax.broadcasted_iota(jnp.int32, (8, LANES), 0)
    group = lane % 4
    nothing = jnp.zeros((8, LANES), f32)
    scale = time_step * damping
    for s in range(2):
        for f in range(FIELDS):
            for t in range(8):
                for a in (0, 1, 18, 19):
                    cells[s, f, a, 8 + 8 * t:16 + 8 * t, :] = nothing

    for copy in smalls:
        copy.wait()
    for d in range(3):
        for f in range(FIELDS):
            for g in range(FIELDS):
                value = jnp.broadcast_to(jac_v[f, d:d + 1, g:g + 1], (8, LANES))
                weights[(d * FIELDS + g) * FIELDS + f] = (-0.5 * time_step) * value
    for f in range(FIELDS):
        for g in range(FIELDS):
            mixes[f * FIELDS + g] = jnp.broadcast_to(mix_v[f:f + 1, g:g + 1], (8, LANES))

    spot = lax.broadcasted_iota(jnp.int32, (24, 256), 1)
    field = sum((spot >= 48 * g).astype(jnp.int32) for g in range(1, FIELDS + 1))
    place = spot - 48 * field
    for block in range(2):
        step = place - lax.broadcasted_iota(jnp.int32, (24, 256), 0) - (8 + 8 * block)
        side = (step == 1).astype(f32) - (step == -1).astype(f32)
        blur = (4.0 * scale) * (jnp.abs(step) == 1).astype(f32) - scale * (jnp.abs(step) == 2).astype(f32)
        for f in range(FIELDS):
            value = jnp.where(field == f, blur, 0.0)
            for g in range(FIELDS):
                weight = jnp.broadcast_to(weights[(FIELDS + g) * FIELDS + f][0:1, 0:1], (24, 256))
                value = value + jnp.where(field == g, weight * side, 0.0)
            high = value.astype(bf16).astype(f32)
            low = value - high
            radial[block, f] = jnp.concatenate([high, low, high], axis=1)

    spare = jnp.zeros((3, LANES), f32)
    blend_rows = jnp.concatenate(
        [part for t in range(TILES) for part in (blend_v[:, LANES * t:LANES * t + LANES], spare)], axis=0
    )
    source_lane = lax.broadcasted_iota(jnp.int32, (LANES, LANES), 0)
    target_lane = lax.broadcasted_iota(jnp.int32, (LANES, LANES), 1)
    chosen = (8 * (source_lane % 16) + source_lane // 16 == target_lane).astype(f32)
    permuted[...] = jnp.dot(
        blend_rows, chosen, precision=lax.Precision.HIGHEST, preferred_element_type=f32
    ).reshape(TILES, 8, LANES)

    def mode_row(k):
        total = nothing
        for t in range(TILES):
            shift = (8 * (t - k)) % LANES
            value = permuted[t]
            total = jnp.where(lane // 8 == t, pltpu.roll(value, shift, 1) if shift else value, total)
        return total

    for c in range(9):
        near = mode_row(c)
        other = mode_row(16 - c) if 0 < c < 8 else nothing
        for f in range(FIELDS):
            blends[c, f, :, 0:LANES] = jnp.broadcast_to(near[f:f + 1, :], (8, LANES))
            blends[c, f, :, LANES:] = jnp.broadcast_to(other[f:f + 1, :], (8, LANES))

    pl.semaphore_wait(barrier, 17)

    def row_copy(s, chunk, target, source):
        first, count = CHUNKS[chunk]
        return pltpu.make_async_remote_copy(
            src_ref=row_block(s, target, first, count), dst_ref=planes.at[s, source, pl.ds(first, count)],
            send_sem=row_send.at[s, chunk, target], recv_sem=row_recv.at[s, chunk, source],
            device_id={"pitch": target}, device_id_type=MESH,
        )

    for chunk in range(len(CHUNKS)):

        for target in targets:
            for s in range(2):
                row_copy(s, chunk, target, me).start()

    def halo_copy(slot, src, dst, where):
        return pltpu.make_async_remote_copy(
            src_ref=src, dst_ref=dst, send_sem=halo_send.at[slot], recv_sem=halo_recv.at[slot],
            device_id=where, device_id_type=MESH,
        )

    to_above = halo_copy(0, span_pack.at[0], span_recv.at[0], {"span": above})
    to_below = halo_copy(1, span_pack.at[1], span_recv.at[1], {"span": below})
    to_right = halo_copy(2, pitch_pack.at[0], pitch_recv.at[0], {"pitch": right})
    to_left = halo_copy(3, pitch_pack.at[1], pitch_recv.at[1], {"pitch": left})

    for s in range(2):
        for f in range(FIELDS):
            load(s, f).wait()

        def pack(pair, carry):
            found = []
            for half in range(2):
                m = 2 * pair + half
                f, first = m // 4, 2 + 4 * (m % 4)
                edge = jnp.zeros((8, LANES), f32)
                low = jnp.zeros((8, LANES), f32)
                high = jnp.zeros((8, LANES), f32)
                for j in range(4):
                    for t in range(8):
                        n = 8 * j + t
                        value = cells[s, f, first + j, 8 + 8 * t:16 + 8 * t, :]
                        edge = jnp.where(lane // 4 == n, pltpu.roll(value, (2 + 4 * n) % LANES, 1), edge)
                        if t == 0:
                            low = jnp.where(row // 2 == j, pltpu.roll(value, 2 * j, 0) if j else value, low)
                        if t == 7:
                            shift = (2 * j + 2) % 8
                            high = jnp.where(row // 2 == j, pltpu.roll(value, shift, 0) if shift else value, high)
                span_pack[0, s, m] = high
                span_pack[1, s, m] = low
                found.append(edge)
            pitch_pack[0, s, pair] = jnp.where(group < 2, found[0], pltpu.roll(found[1], 2, 1))
            pitch_pack[1, s, pair] = jnp.where(group < 2, pltpu.roll(found[0], LANES - 2, 1), found[1])
            return carry

        lax.fori_loop(0, 10, pack, 0)
    for copy in (to_above, to_below, to_right, to_left):
        copy.start()

    def base_ghosts(block, carry):
        rows = pl.ds(pl.multiple_of(8 + 8 * block, 8), 8)
        for s in range(2):
            for layer in range(2):
                kept = [cells[s, g, 17 - layer if s == 0 else 2 + layer, rows, :] for g in range(FIELDS)]
                for f in range(FIELDS):
                    total = mixes[f * FIELDS] * kept[0]
                    for g in range(1, FIELDS):
                        total = total + mixes[f * FIELDS + g] * kept[g]
                    cells[s, f, 18 + layer if s == 0 else 1 - layer, rows, :] = total
        return carry

    lax.fori_loop(0, 8, base_ghosts, 0)

    rim = (lane < 2) | (lane >= LANES - 2)

    def products(layer, bent, rows_out):
        highs, lows = [], []
        for k in range(2):
            s, a = (layer + k) // AX, (layer + k) % AX
            values = cells[s, :, a + 2, 8:8 + ROWS, :].reshape(FIELDS * ROWS, LANES)
            high = values.astype(bf16)
            low = (values - high.astype(f32)).astype(bf16)
            both = jnp.concatenate([high, low], axis=1)
            bent[k] = jnp.dot(both, band_ref[...], preferred_element_type=f32).reshape(FIELDS, ROWS, 256)
            highs.append(high)
            lows.append(low)
        blank = jnp.zeros((16, LANES), bf16)
        for block in range(2):

            def stacked(parts):
                return jnp.concatenate([
                    jnp.concatenate(
                        [part[ROWS * g + 16 * block:ROWS * g + 16 * block + 48, :] for g in range(FIELDS)] + [blank], axis=0
                    )
                    for part in parts
                ], axis=1)

            upper = stacked(highs)
            data = jnp.concatenate([upper, upper, stacked(lows)], axis=0)
            left = radial[block].reshape(FIELDS * 24, 768).astype(bf16)
            rows_out[block] = jnp.dot(left, data, preferred_element_type=f32).reshape(FIELDS, 24, 256)

    def pitch_fix(s, f, a, tile):
        amount = lax.rem(126 - 32 * lax.rem(a, 4) - 4 * tile + 2 * LANES, LANES)
        return jnp.where(rim, pltpu.roll(edge_fix[s, f, a // 4], amount, 1), 0.0)

    def sweep(layer, first, rows, bent, fixed):
        s, a = layer // AX, layer % AX
        count = rows // 8
        sums = [None] * FIELDS
        for g in range(FIELDS):

            def get(axial, radial):
                start = 8 + first + radial
                return cells[s, g, a + 2 + axial, start:start + rows, :].reshape(count, 8, LANES)

            ahead, behind = get(1, 0), get(-1, 0)
            up, down = get(0, 1), get(0, -1)
            near = (ahead + behind) + (up + down)
            far = (get(2, 0) + get(-2, 0)) + (get(0, 2) + get(0, -2))
            own = bent(g)[:, LANES:].reshape(count, 8, LANES) + ((4.0 * scale) * near - scale * far)
            along = bent(g)[:, 0:LANES].reshape(count, 8, LANES)
            if fixed:
                own = own + jnp.stack([pitch_fix(s, g, a, first // 8 + t) for t in range(count)])
            sums[g] = own if sums[g] is None else sums[g] + own
            for d, slope in enumerate((ahead - behind, up - down, along)):
                for f in range(FIELDS):
                    term = weights[(d * FIELDS + g) * FIELDS + f] * slope
                    sums[f] = term if sums[f] is None else sums[f] + term
        for f in range(FIELDS):
            partial[s, f, a, first:first + rows, :] = sums[f].reshape(rows, LANES)

    def inner(layer, k, bent, rows_in, fixed):
        s, a = layer // AX, layer % AX
        sums = [
            jnp.concatenate([rows_in[block, f, :, LANES * k:LANES * k + LANES] for block in range(2)], axis=0).reshape(6, 8, LANES)
            for f in range(FIELDS)
        ]
        for g in range(FIELDS):

            def get(axial):
                return cells[s, g, a + 2 + axial, 16:8 + ROWS - 8, :].reshape(6, 8, LANES)

            ahead, behind = get(1), get(-1)
            along = bent[k, g, 8:ROWS - 8, 0:LANES].reshape(6, 8, LANES)
            own = bent[k, g, 8:ROWS - 8, LANES:].reshape(6, 8, LANES)
            own = own + ((4.0 * scale) * (ahead + behind) - scale * (get(2) + get(-2)))
            if fixed:
                own = own + jnp.stack([pitch_fix(s, g, a, 1 + t) for t in range(6)])
            sums[g] = sums[g] + own
            for d, slope in ((0, ahead - behind), (2, along)):
                for f in range(FIELDS):
                    sums[f] = sums[f] + weights[(d * FIELDS + g) * FIELDS + f] * slope
        for f in range(FIELDS):
            partial[s, f, a, 8:ROWS - 8, :] = sums[f].reshape(48, LANES)

    def early_layer(layer, k, bent, rows_in):
        inner(layer, k, bent, rows_in, False)
        kept[layer, :, 0:8, :] = bent[k, :, 0:8, :]
        kept[layer, :, 8:16, :] = bent[k, :, ROWS - 8:, :]

    def late_layer(layer, k, bent, rows_in):
        inner(layer, k, bent, rows_in, True)
        sweep(layer, 0, 8, lambda g: bent[k, g, 0:8, :], True)
        sweep(layer, ROWS - 8, 8, lambda g: bent[k, g, ROWS - 8:, :], True)

    def finish_early(layer, carry):
        s, a = layer // AX, layer % AX
        sweep(layer, 0, 8, lambda g: kept[layer, g, 0:8, :], True)
        sweep(layer, ROWS - 8, 8, lambda g: kept[layer, g, 8:16, :], True)
        for f in range(FIELDS):
            for t in range(1, 7):
                partial[s, f, a, 8 * t:8 * t + 8, :] = partial[s, f, a, 8 * t:8 * t + 8, :] + pitch_fix(s, f, a, t)
        return carry

    def layers(first, last, step):
        products(first, bent_a, rows_a)

        def four_layers(i, carry):
            products(4 * i + 2, bent_b, rows_b)
            step(4 * i, 0, bent_a, rows_a)
            step(4 * i + 1, 1, bent_a, rows_a)
            products(jnp.minimum(4 * i + 4, last - 2), bent_a, rows_a)
            step(4 * i + 2, 0, bent_b, rows_b)
            step(4 * i + 3, 1, bent_b, rows_b)
            return carry

        lax.fori_loop(first // 4, last // 4, four_layers, 0)


    offset = off_ref[0]
    shift, hop = lax.rem(offset, LANES), offset // LANES

    for s in range(2):
        own_rows(s).wait()

    def back_copy(chunk, target, source):
        first, count = CHUNKS[chunk]
        return pltpu.make_async_remote_copy(
            src_ref=outgoing.at[target, :, pl.ds(first, count)], dst_ref=ghost_ref.at[source, :, pl.ds(first, count)],
            send_sem=back_send.at[chunk, target], recv_sem=back_recv.at[chunk, source],
            device_id={"pitch": target}, device_id_type=MESH,
        )

    for chunk, (start, count) in enumerate(CHUNKS):
        done = sum(BEFORE[:chunk])
        if BEFORE[chunk]:
            layers(done, done + BEFORE[chunk], early_layer)

        def turn(source):
            for f in range(start, start + count):
                turned[source, f] = pltpu.roll(planes[1, source, f], shift, 1)

        turn(me)
        for source in sources:
            for s in range(2):
                row_copy(s, chunk, source, source).wait_recv()
            turn(source)

        def forward(f, carry):
            x = []
            for t in range(TILES):
                near = turned[lax.rem(t + 16 - hop, 16), f]
                far = turned[lax.rem(t + 15 - hop, 16), f]
                x.append(jnp.where(lane >= shift, near, far) - planes[0, t, f])
            cs, ss = forward_16(x)
            for c in range(9):
                cosines, sines = twiddle_ref[0, c], twiddle_ref[1, c]
                if c == 0:
                    real, imaginary = cs[0], nothing
                elif c == 8:
                    real, imaginary = cs[8] * cosines, -(cs[8] * sines)
                else:
                    real = cs[c] * cosines - ss[c] * sines
                    imaginary = -(cs[c] * sines + ss[c] * cosines)
                spectrum[c, f, :, 0:LANES] = real
                spectrum[c, f, :, LANES:] = imaginary
            return carry

        lax.fori_loop(start, start + count, forward, 0, unroll=True)
        modes = split_dot(spectrum[:, start:start + count].reshape(72 * count, 256), table_ref)
        modes = modes * blends[:, start:start + count].reshape(72 * count, 256)
        spectrum[:, start:start + count] = split_dot(modes, back_ref).reshape(9, count, 8, 256)

        def inverse(f, carry):
            cs, ss = [], []
            for c in range(9):
                cosines, sines = twiddle_ref[0, c], twiddle_ref[1, c]
                real, imaginary = spectrum[c, f, :, 0:LANES], spectrum[c, f, :, LANES:]
                cs.append(real * cosines - imaginary * sines)
                ss.append(-(real * sines + imaginary * cosines))
            x = inverse_16(cs, ss)
            for t in range(TILES):
                outgoing[t, 0, f] = x[t]
                turned[t, f] = pltpu.roll(x[t], lax.rem(LANES - shift, LANES), 1)
            for t in range(TILES):
                near = turned[lax.rem(t + hop, 16), f]
                far = turned[lax.rem(t + hop + 1, 16), f]
                outgoing[t, 1, f] = jnp.where(lane < LANES - shift, near, far)
            return carry

        lax.fori_loop(start, start + count, inverse, 0, unroll=True)

        for target in targets:
            back_copy(chunk, target, me).start()

    own_back = pltpu.make_async_copy(outgoing.at[me], ghost_ref.at[me], own_sem.at[0])
    own_back.start()

    for copy in (to_above, to_below, to_right, to_left):
        copy.wait()
    keep_low = jnp.where(span == 0, 0.0, 1.0).astype(f32)
    keep_high = jnp.where(span == 7, 0.0, 1.0).astype(f32)
    for s in range(2):

        def unpack(m, carry):
            f, first = m // 4, 4 * (m % 4)
            low = span_recv[0, s, m] * keep_low
            high = span_recv[1, s, m] * keep_high
            for j in range(4):
                cells[s, f, 2 + first + j, 6:8, :] = low[2 * j:2 * j + 2, :]
                cells[s, f, 2 + first + j, 72:74, :] = high[2 * j:2 * j + 2, :]
            return carry

        lax.fori_loop(0, 20, unpack, 0)

        def edges(quarter_pair, carry):
            total = [[None] * FIELDS, [None] * FIELDS]
            for g in range(FIELDS):
                from_left, from_right = pitch_recv[0, s, 2 * g + quarter_pair], pitch_recv[1, s, 2 * g + quarter_pair]
                for half in range(2):
                    if half == 0:
                        halo = jnp.where(group < 2, from_left, pltpu.roll(from_right, 2, 1))
                    else:
                        halo = jnp.where(group < 2, pltpu.roll(from_left, LANES - 2, 1), from_right)
                    plus_1, minus_1 = pltpu.roll(halo, LANES - 1, 1), pltpu.roll(halo, 1, 1)
                    plus_2, minus_2 = pltpu.roll(halo, LANES - 2, 1), pltpu.roll(halo, 2, 1)
                    slope = jnp.where(group == 1, plus_1, jnp.where(group == 2, -minus_1, 0.0))
                    smooth = jnp.where(group < 2, plus_2, minus_2) - 4.0 * jnp.where(
                        group == 1, plus_1, jnp.where(group == 2, minus_1, 0.0)
                    )
                    for f in range(FIELDS):
                        term = weights[(2 * FIELDS + g) * FIELDS + f] * slope
                        if f == g:
                            term = term - scale * smooth
                        total[half][f] = term if total[half][f] is None else total[half][f] + term
            for half in range(2):
                for f in range(FIELDS):
                    edge_fix[s, f, 2 * quarter_pair + half] = total[half][f]
            return carry

        lax.fori_loop(0, 2, edges, 0)

    layers(EARLY, 2 * AX, late_layer)
    lax.fori_loop(0, EARLY, finish_early, 0)

    own_back.wait()

    def finish(j, carry):
        other = lax.rem(me + j, 16)
        for chunk in range(len(CHUNKS)):
            for s in range(2):
                row_copy(s, chunk, other, me).wait_send()
            back_copy(chunk, other, me).wait_send()
            back_copy(chunk, other, other).wait_recv()
        return carry

    lax.fori_loop(1, 16, finish, 0)


def band_table():
    position = np.arange(LANES)
    scale = time_step * damping
    slope = np.zeros((LANES, LANES))
    smooth = np.zeros((LANES, LANES))
    for step, weight in ((1, 1.0), (-1, -1.0)):
        inside = position[(position + step >= 0) & (position + step < LANES)]
        slope[inside + step, inside] += weight
    for step, weight in ((0, 1.0 - 18.0 * scale), (1, 4.0 * scale), (-1, 4.0 * scale), (2, -scale), (-2, -scale)):
        inside = position[(position + step >= 0) & (position + step < LANES)]
        smooth[inside + step, inside] += weight
    table = np.concatenate([slope, smooth], axis=1)
    return np.concatenate([table, table], axis=0).astype(ml_dtypes.bfloat16)


def section(offset, stator, rotor, blend, jacobians, field_mix):
    forward_table, back_table, twiddle = transform_tables()
    whole = pl.BlockSpec(memory_space=pltpu.VMEM)
    anywhere = pl.BlockSpec(memory_space=pl.ANY)
    dma = pltpu.SemaphoreType.DMA
    return pl.pallas_call(
        section_kernel,
        name="section",
        out_shape=(
            pltpu.VMEM((2, FIELDS, AX, ROWS, LANES), f32),
            pltpu.VMEM((16, 2, FIELDS, 8, LANES), f32),
            pltpu.VMEM((75, 8, LANES), f32),
            pltpu.VMEM((25, 8, LANES), f32),
        ),
        in_specs=[pl.BlockSpec(memory_space=pltpu.SMEM)] + [pl.BlockSpec(memory_space=pltpu.HBM)] * 9,
        out_specs=(whole, whole, whole, whole),
        scratch_shapes=[
            pltpu.VMEM((2, FIELDS, AX + 4, ROWS + 16, LANES), f32),
            pltpu.VMEM((2, 16, FIELDS, 8, LANES), f32),
            pltpu.VMEM((9, FIELDS, 8, 256), f32),
            pltpu.VMEM((9, FIELDS, 8, 256), f32),
            pltpu.VMEM((16, FIELDS, 8, LANES), f32),
            pltpu.VMEM((16, 2, FIELDS, 8, LANES), f32),
            pltpu.VMEM((2, 2, 10, 8, LANES), f32),
            pltpu.VMEM((2, 2, 10, 8, LANES), f32),
            pltpu.VMEM((2, 2, 20, 8, LANES), f32),
            pltpu.VMEM((2, 2, 20, 8, LANES), f32),
            pltpu.VMEM((2, FIELDS, ROWS, 256), f32),
            pltpu.VMEM((2, FIELDS, ROWS, 256), f32),
            pltpu.VMEM((2, FIELDS, 24, 256), f32),
            pltpu.VMEM((2, FIELDS, 24, 256), f32),
            pltpu.VMEM((2, FIELDS, 24, 768), f32),
            pltpu.VMEM((EARLY, FIELDS, 16, 256), f32),
            pltpu.VMEM((2, FIELDS, 4, 8, LANES), f32),
            pltpu.VMEM((TILES, 8, LANES), f32),
            pltpu.VMEM((FIELDS, NP), f32),
            pltpu.VMEM((FIELDS, 3, FIELDS), f32),
            pltpu.VMEM((FIELDS, FIELDS), f32),
            pltpu.VMEM((2, 256, 256), bf16),
            pltpu.VMEM((2, 256, 256), bf16),
            pltpu.VMEM((2, 9, 1, LANES), f32),
            pltpu.VMEM((256, 256), bf16),
            dma((2, FIELDS)), dma((2,)), dma((2, len(CHUNKS), 16)), dma((2, len(CHUNKS), 16)), dma((len(CHUNKS), 16)), dma((len(CHUNKS), 16)),
            dma((4,)), dma((4,)), dma((7,)),
        ],
        compiler_params=pltpu.CompilerParams(
            collective_id=0, has_side_effects=True, vmem_limit_bytes=32 << 20
        ),
    )(offset, *(
        pltpu.with_memory_space_constraint(jnp.asarray(x), pltpu.HBM)
        for x in (
            stator, rotor, blend, jacobians.transpose(1, 0, 2), field_mix,
            forward_table, back_table, twiddle, band_table(),
        )
    ))


def close_kernel(partial, ghosts, weights, mixes, st_out, ro_out, ends, store_sem, end_sem):
    outs = (st_out, ro_out)
    scale = time_step * damping
    copies = []
    for s in range(2):
        first = 0 if s == 0 else 2
        for f in range(FIELDS):
            copies.append(pltpu.make_async_copy(
                partial.at[s, f, pl.ds(first, AX - 2)], outs[s].at[f, pl.ds(first, AX - 2)], store_sem.at[s, f]
            ))
    for copy in copies:
        copy.start()

    for s in range(2):

        def fill(block, carry):
            rows = pl.ds(pl.multiple_of(8 * block, 8), 8)
            mixed = []
            for layer in range(2):
                parts = [ghosts[8 * layer + block, s, g] for g in range(FIELDS)]
                found = []
                for f in range(FIELDS):
                    total = mixes[f * FIELDS] * parts[0]
                    for g in range(1, FIELDS):
                        total = total + mixes[f * FIELDS + g] * parts[g]
                    found.append(total if s == 0 else -total)
                mixed.append(found)
            outer, inner = (15, 14) if s == 0 else (0, 1)
            for f in range(FIELDS):
                total = (4.0 * scale) * mixed[0][f] - scale * mixed[1][f]
                for g in range(FIELDS):
                    term = weights[g * FIELDS + f] * mixed[0][g]
                    total = total + term if s == 0 else total - term
                ends[s, f, outer % 2, rows, :] = partial[s, f, outer, rows, :] + total
                ends[s, f, inner % 2, rows, :] = partial[s, f, inner, rows, :] - scale * mixed[0][f]
            return carry

        lax.fori_loop(0, 8, fill, 0)
        last = pltpu.make_async_copy(ends.at[s], outs[s].at[:, pl.ds(14 if s == 0 else 0, 2)], end_sem.at[s])
        last.start()
        copies.append(last)
    for copy in copies:
        copy.wait()


def close(partial, ghosts, weights, mixes):
    anywhere = pl.BlockSpec(memory_space=pl.ANY)
    whole = pl.BlockSpec(memory_space=pltpu.VMEM)
    dma = pltpu.SemaphoreType.DMA
    shape = jax.ShapeDtypeStruct((FIELDS, AX, ROWS, LANES), f32)
    return pl.pallas_call(
        close_kernel,
        name="close",
        out_shape=(shape, shape),
        in_specs=[whole] * 4,
        out_specs=(anywhere, anywhere),
        scratch_shapes=[pltpu.VMEM((2, FIELDS, 2, ROWS, LANES), f32), dma((2, FIELDS)), dma((2,))],
        compiler_params=pltpu.CompilerParams(vmem_limit_bytes=8 << 20),
    )(partial, ghosts, weights, mixes)


def shards(stator_state, rotor_state, jacobians, field_mix, mode_blend, rotor_offset):
    parts = section(rotor_offset, stator_state, rotor_state, mode_blend, jacobians, field_mix)
    return close(*parts)


def solution(mesh):
    in_specs = (P(None, None, "span", "pitch"), P(None, None, "span", "pitch"), P(), P(), P(), P())
    out_specs = (P(None, None, "span", "pitch"), P(None, None, "span", "pitch"))
    return jax.shard_map(shards, mesh=mesh, in_specs=in_specs, out_specs=out_specs, check_vma=False)
```

```python
import math

import jax
import jax.numpy as jnp
import ml_dtypes
import numpy as np
from jax import lax
from jax.experimental import pallas as pl
from jax.experimental.pallas import tpu as pltpu
from jax.sharding import PartitionSpec as P

NP = 2048
FIELDS = 5
AX = 16
ROWS = 64
LANES = 128
TILES = 16
MESH = pl.DeviceIdType.MESH
EARLY = 12
BEFORE = (12,)
CHUNKS = ((0, 5),)
ORDER = (
    (2, 2), (2, 3), (3, 2), (2, 1), (1, 2), (2, 0), (0, 2), (3, 1), (1, 3), (3, 3), (1, 1), (3, 0), (0, 3), (1, 0), (0, 1),
)
f32 = jnp.float32
bf16 = jnp.bfloat16

time_step = 0.5
damping = 1.0 / 32.0


def transform_tables():
    q = np.arange(LANES)
    w = 2.0 * np.pi / LANES

    def cas(m):
        angle = w * (m % LANES)
        return np.cos(angle) + np.sin(angle)

    first, second = np.outer(q, q), np.outer(q, q + 1)
    table = np.block([[cas(first), cas(second)], [-cas(-first), cas(-second)]])

    def parts(array):
        array = array.astype(np.float32)
        high = array.astype(ml_dtypes.bfloat16)
        low = (array - high.astype(np.float32)).astype(ml_dtypes.bfloat16)
        return np.stack([high, low])

    psi = 2.0 * np.pi * np.outer(np.arange(9), q) / NP
    twiddle = np.stack([np.cos(psi), np.sin(psi)]).astype(np.float32)
    return parts(table), parts(table.T / NP), twiddle[:, :, None, :]


def cosine(m):
    return math.cos(2.0 * math.pi * (m % 16) / 16)


def sine(m):
    return math.sin(2.0 * math.pi * (m % 16) / 16)


def weighted(terms):
    total = None
    for weight, value in terms:
        if abs(weight) < 1e-9:
            continue
        if abs(weight - 1.0) < 1e-9:
            total = value if total is None else total + value
        elif abs(weight + 1.0) < 1e-9:
            total = -value if total is None else total - value
        else:
            total = weight * value if total is None else total + weight * value
    return total


def forward_16(x):
    e = [None] + [x[p] + x[16 - p] for p in range(1, 8)]
    o = [None] + [x[p] - x[16 - p] for p in range(1, 8)]
    x_even, x_odd = x[0] + x[8], x[0] - x[8]
    ee = [None] + [e[p] + e[8 - p] for p in range(1, 4)]
    eo = [None] + [e[p] - e[8 - p] for p in range(1, 4)]
    oo = [None] + [o[p] + o[8 - p] for p in range(1, 4)]
    oe = [None] + [o[p] - o[8 - p] for p in range(1, 4)]
    cs, ss = [], []
    for c in range(9):
        if c % 2 == 0:
            cs.append(weighted([(1.0, x_even), (cosine(4 * c), e[4])] + [(cosine(p * c), ee[p]) for p in range(1, 4)]))
            ss.append(weighted([(sine(p * c), oe[p]) for p in range(1, 4)]) if 0 < c < 8 else None)
        else:
            cs.append(weighted([(1.0, x_odd)] + [(cosine(p * c), eo[p]) for p in range(1, 4)]))
            ss.append(weighted([(sine(4 * c), o[4])] + [(sine(p * c), oo[p]) for p in range(1, 4)]))
    return cs, ss


def inverse_16(cs, ss):
    x = [None] * 16
    x[0] = weighted([(1.0, v) for v in cs])
    x[8] = weighted([((-1.0) ** c, v) for c, v in enumerate(cs)])
    for p in range(1, 5):
        ev = weighted([(1.0, cs[0]), (cosine(8 * p), cs[8])] + [(cosine(p * c), cs[c]) for c in range(2, 8, 2)])
        eo = weighted([(cosine(p * c), cs[c]) for c in range(1, 8, 2)])
        ov = weighted([(sine(p * c), ss[c]) for c in range(2, 8, 2)])
        oo = weighted([(sine(p * c), ss[c]) for c in range(1, 8, 2)])
        if p == 4:
            x[4], x[12] = ev + oo, ev - oo
            continue
        x[p] = (ev + eo) + (ov + oo)
        x[16 - p] = (ev + eo) - (ov + oo)
        x[8 - p] = (ev - eo) + (oo - ov)
        x[8 + p] = (ev - eo) - (oo - ov)
    return x


def split_dot(values, table_ref):
    high = values.astype(bf16)
    low = (values - high.astype(f32)).astype(bf16)

    def dot(left, right):
        return jnp.dot(left, right, preferred_element_type=f32)

    return dot(high, table_ref[0]) + dot(low, table_ref[0]) + dot(high, table_ref[1])


def section_kernel(
    off_ref, st_ref, ro_ref, blend_hbm, jac_hbm, mix_hbm, table_hbm, back_hbm, twiddle_hbm, band_hbm,
    partial, ghost_ref, weights, mixes,
    cells, planes, spectrum, blends, turned, outgoing, pitch_pack, pitch_recv, span_pack, span_recv,
    bent_a, bent_b, rows_a, rows_b, radial, kept, edge_fix, permuted, blend_v, jac_v, mix_v, table_ref, back_ref, twiddle_ref, band_ref,
    load_sem, own_sem, row_send, row_recv, back_send, back_recv, halo_send, halo_recv, small_sem,
):
    me = lax.axis_index("pitch")
    span = lax.axis_index("span")
    left, right = lax.rem(me + 15, 16), lax.rem(me + 1, 16)
    targets = [4 * lax.rem(me // 4 + dx, 4) + lax.rem(me + dz, 4) for dx, dz in ORDER]
    sources = [4 * lax.rem(me // 4 + 4 - dx, 4) + lax.rem(me + 4 - dz, 4) for dx, dz in ORDER]
    below, above = lax.rem(span + 7, 8), lax.rem(span + 1, 8)
    states = (st_ref, ro_ref)

    def load(s, f):
        return pltpu.make_async_copy(states[s].at[f], cells.at[s, f, pl.ds(2, AX), pl.ds(8, ROWS)], load_sem.at[s, f])

    def row_block(s, target, first=0, count=FIELDS):
        layer, block = target // 8, target % 8
        axial = 15 - layer if s == 0 else layer
        rows = pl.ds(pl.multiple_of(8 * block, 8), 8)
        return states[s].at[pl.ds(first, count), axial, rows, :]

    def own_rows(s):
        return pltpu.make_async_copy(row_block(s, me), planes.at[s, me], own_sem.at[s])

    barrier = pltpu.get_barrier_semaphore()

    def greet(j, carry):
        pl.semaphore_signal(barrier, inc=1, device_id={"pitch": lax.rem(me + j, 16)}, device_id_type=MESH)
        return carry

    lax.fori_loop(1, 16, greet, 0)
    for other in (below, above):
        pl.semaphore_signal(barrier, inc=1, device_id={"span": other}, device_id_type=MESH)

    smalls = [
        pltpu.make_async_copy(source, target, small_sem.at[i])
        for i, (source, target) in enumerate((
            (blend_hbm, blend_v), (jac_hbm, jac_v), (mix_hbm, mix_v),
            (table_hbm, table_ref), (back_hbm, back_ref), (twiddle_hbm, twiddle_ref), (band_hbm, band_ref),
        ))
    ]
    for s in range(2):
        own_rows(s).start()
    for s in range(2):
        for f in range(FIELDS):
            load(s, f).start()
    for copy in smalls:
        copy.start()

    lane = lax.broadcasted_iota(jnp.int32, (8, LANES), 1)
    row = lax.broadcasted_iota(jnp.int32, (8, LANES), 0)
    group = lane % 4
    nothing = jnp.zeros((8, LANES), f32)
    scale = time_step * damping
    for s in range(2):
        for f in range(FIELDS):
            for t in range(8):
                for a in (0, 1, 18, 19):
                    cells[s, f, a, 8 + 8 * t:16 + 8 * t, :] = nothing

    for copy in smalls:
        copy.wait()
    for d in range(3):
        for f in range(FIELDS):
            for g in range(FIELDS):
                value = jnp.broadcast_to(jac_v[f, d:d + 1, g:g + 1], (8, LANES))
                weights[(d * FIELDS + g) * FIELDS + f] = (-0.5 * time_step) * value
    for f in range(FIELDS):
        for g in range(FIELDS):
            mixes[f * FIELDS + g] = jnp.broadcast_to(mix_v[f:f + 1, g:g + 1], (8, LANES))

    spot = lax.broadcasted_iota(jnp.int32, (24, 256), 1)
    field = sum((spot >= 48 * g).astype(jnp.int32) for g in range(1, FIELDS + 1))
    place = spot - 48 * field
    for block in range(2):
        step = place - lax.broadcasted_iota(jnp.int32, (24, 256), 0) - (8 + 8 * block)
        side = (step == 1).astype(f32) - (step == -1).astype(f32)
        blur = (4.0 * scale) * (jnp.abs(step) == 1).astype(f32) - scale * (jnp.abs(step) == 2).astype(f32)
        for f in range(FIELDS):
            value = jnp.where(field == f, blur, 0.0)
            for g in range(FIELDS):
                weight = jnp.broadcast_to(weights[(FIELDS + g) * FIELDS + f][0:1, 0:1], (24, 256))
                value = value + jnp.where(field == g, weight * side, 0.0)
            high = value.astype(bf16).astype(f32)
            low = value - high
            radial[block, f] = jnp.concatenate([high, low, high], axis=1)

    spare = jnp.zeros((3, LANES), f32)
    blend_rows = jnp.concatenate(
        [part for t in range(TILES) for part in (blend_v[:, LANES * t:LANES * t + LANES], spare)], axis=0
    )
    source_lane = lax.broadcasted_iota(jnp.int32, (LANES, LANES), 0)
    target_lane = lax.broadcasted_iota(jnp.int32, (LANES, LANES), 1)
    chosen = (8 * (source_lane % 16) + source_lane // 16 == target_lane).astype(f32)
    permuted[...] = jnp.dot(
        blend_rows, chosen, precision=lax.Precision.HIGHEST, preferred_element_type=f32
    ).reshape(TILES, 8, LANES)

    def mode_row(k):
        total = nothing
        for t in range(TILES):
            shift = (8 * (t - k)) % LANES
            value = permuted[t]
            total = jnp.where(lane // 8 == t, pltpu.roll(value, shift, 1) if shift else value, total)
        return total

    for c in range(9):
        near = mode_row(c)
        other = mode_row(16 - c) if 0 < c < 8 else nothing
        for f in range(FIELDS):
            blends[c, f, :, 0:LANES] = jnp.broadcast_to(near[f:f + 1, :], (8, LANES))
            blends[c, f, :, LANES:] = jnp.broadcast_to(other[f:f + 1, :], (8, LANES))

    pl.semaphore_wait(barrier, 17)

    def row_copy(s, chunk, target, source):
        first, count = CHUNKS[chunk]
        return pltpu.make_async_remote_copy(
            src_ref=row_block(s, target, first, count), dst_ref=planes.at[s, source, pl.ds(first, count)],
            send_sem=row_send.at[s, chunk, target], recv_sem=row_recv.at[s, chunk, source],
            device_id={"pitch": target}, device_id_type=MESH,
        )

    for chunk in range(len(CHUNKS)):

        for target in targets:
            for s in range(2):
                row_copy(s, chunk, target, me).start()

    def halo_copy(slot, src, dst, where):
        return pltpu.make_async_remote_copy(
            src_ref=src, dst_ref=dst, send_sem=halo_send.at[slot], recv_sem=halo_recv.at[slot],
            device_id=where, device_id_type=MESH,
        )

    to_above = halo_copy(0, span_pack.at[0], span_recv.at[0], {"span": above})
    to_below = halo_copy(1, span_pack.at[1], span_recv.at[1], {"span": below})
    to_right = halo_copy(2, pitch_pack.at[0], pitch_recv.at[0], {"pitch": right})
    to_left = halo_copy(3, pitch_pack.at[1], pitch_recv.at[1], {"pitch": left})

    for s in range(2):
        for f in range(FIELDS):
            load(s, f).wait()

        def pack(pair, carry):
            found = []
            for half in range(2):
                m = 2 * pair + half
                f, first = m // 4, 2 + 4 * (m % 4)
                edge = jnp.zeros((8, LANES), f32)
                low = jnp.zeros((8, LANES), f32)
                high = jnp.zeros((8, LANES), f32)
                for j in range(4):
                    for t in range(8):
                        n = 8 * j + t
                        value = cells[s, f, first + j, 8 + 8 * t:16 + 8 * t, :]
                        edge = jnp.where(lane // 4 == n, pltpu.roll(value, (2 + 4 * n) % LANES, 1), edge)
                        if t == 0:
                            low = jnp.where(row // 2 == j, pltpu.roll(value, 2 * j, 0) if j else value, low)
                        if t == 7:
                            shift = (2 * j + 2) % 8
                            high = jnp.where(row // 2 == j, pltpu.roll(value, shift, 0) if shift else value, high)
                span_pack[0, s, m] = high
                span_pack[1, s, m] = low
                found.append(edge)
            pitch_pack[0, s, pair] = jnp.where(group < 2, found[0], pltpu.roll(found[1], 2, 1))
            pitch_pack[1, s, pair] = jnp.where(group < 2, pltpu.roll(found[0], LANES - 2, 1), found[1])
            return carry

        lax.fori_loop(0, 10, pack, 0)
    for copy in (to_above, to_below, to_right, to_left):
        copy.start()

    def base_ghosts(block, carry):
        rows = pl.ds(pl.multiple_of(8 + 8 * block, 8), 8)
        for s in range(2):
            for layer in range(2):
                kept = [cells[s, g, 17 - layer if s == 0 else 2 + layer, rows, :] for g in range(FIELDS)]
                for f in range(FIELDS):
                    total = mixes[f * FIELDS] * kept[0]
                    for g in range(1, FIELDS):
                        total = total + mixes[f * FIELDS + g] * kept[g]
                    cells[s, f, 18 + layer if s == 0 else 1 - layer, rows, :] = total
        return carry

    lax.fori_loop(0, 8, base_ghosts, 0)

    rim = (lane < 2) | (lane >= LANES - 2)

    def products(layer, bent, rows_out):
        highs, lows = [], []
        for k in range(2):
            s, a = (layer + k) // AX, (layer + k) % AX
            values = cells[s, :, a + 2, 8:8 + ROWS, :].reshape(FIELDS * ROWS, LANES)
            high = values.astype(bf16)
            low = (values - high.astype(f32)).astype(bf16)
            both = jnp.concatenate([high, low], axis=1)
            bent[k] = jnp.dot(both, band_ref[...], preferred_element_type=f32).reshape(FIELDS, ROWS, 256)
            highs.append(high)
            lows.append(low)
        blank = jnp.zeros((16, LANES), bf16)
        for block in range(2):

            def stacked(parts):
                return jnp.concatenate([
                    jnp.concatenate(
                        [part[ROWS * g + 16 * block:ROWS * g + 16 * block + 48, :] for g in range(FIELDS)] + [blank], axis=0
                    )
                    for part in parts
                ], axis=1)

            upper = stacked(highs)
            data = jnp.concatenate([upper, upper, stacked(lows)], axis=0)
            left = radial[block].reshape(FIELDS * 24, 768).astype(bf16)
            rows_out[block] = jnp.dot(left, data, preferred_element_type=f32).reshape(FIELDS, 24, 256)

    def pitch_fix(s, f, a, tile):
        amount = lax.rem(126 - 32 * lax.rem(a, 4) - 4 * tile + 2 * LANES, LANES)
        return jnp.where(rim, pltpu.roll(edge_fix[s, f, a // 4], amount, 1), 0.0)

    def rim_tiles(layer, bent):
        s, a = layer // AX, layer % AX
        sums = [None] * FIELDS
        for g in range(FIELDS):

            def get(axial, radial):
                low, high = 8 + radial, ROWS + radial
                return jnp.stack([
                    cells[s, g, a + 2 + axial, low:low + 8, :], cells[s, g, a + 2 + axial, high:high + 8, :],
                ])

            ahead, behind = get(1, 0), get(-1, 0)
            up, down = get(0, 1), get(0, -1)
            near = (ahead + behind) + (up + down)
            far = (get(2, 0) + get(-2, 0)) + (get(0, 2) + get(0, -2))
            pitch = bent(g)
            along = pitch[:, 0:LANES].reshape(2, 8, LANES)
            own = pitch[:, LANES:].reshape(2, 8, LANES) + ((4.0 * scale) * near - scale * far)
            own = own + jnp.stack([pitch_fix(s, g, a, 0), pitch_fix(s, g, a, 7)])
            sums[g] = own if sums[g] is None else sums[g] + own
            for d, slope in enumerate((ahead - behind, up - down, along)):
                for f in range(FIELDS):
                    term = weights[(d * FIELDS + g) * FIELDS + f] * slope
                    sums[f] = term if sums[f] is None else sums[f] + term
        for f in range(FIELDS):
            partial[s, f, a, 0:8, :] = sums[f][0]
            partial[s, f, a, ROWS - 8:ROWS, :] = sums[f][1]

    def inner(layer, k, bent, rows_in, fixed):
        s, a = layer // AX, layer % AX
        sums = [
            jnp.concatenate([rows_in[block, f, :, LANES * k:LANES * k + LANES] for block in range(2)], axis=0).reshape(6, 8, LANES)
            for f in range(FIELDS)
        ]
        for g in range(FIELDS):

            def get(axial):
                return cells[s, g, a + 2 + axial, 16:8 + ROWS - 8, :].reshape(6, 8, LANES)

            ahead, behind = get(1), get(-1)
            along = bent[k, g, 8:ROWS - 8, 0:LANES].reshape(6, 8, LANES)
            own = bent[k, g, 8:ROWS - 8, LANES:].reshape(6, 8, LANES)
            own = own + ((4.0 * scale) * (ahead + behind) - scale * (get(2) + get(-2)))
            if fixed:
                own = own + jnp.stack([pitch_fix(s, g, a, 1 + t) for t in range(6)])
            sums[g] = sums[g] + own
            for d, slope in ((0, ahead - behind), (2, along)):
                for f in range(FIELDS):
                    sums[f] = sums[f] + weights[(d * FIELDS + g) * FIELDS + f] * slope
        for f in range(FIELDS):
            partial[s, f, a, 8:ROWS - 8, :] = sums[f].reshape(48, LANES)

    def early_layer(layer, k, bent, rows_in):
        inner(layer, k, bent, rows_in, False)
        kept[layer, :, 0:8, :] = bent[k, :, 0:8, :]
        kept[layer, :, 8:16, :] = bent[k, :, ROWS - 8:, :]

    def late_layer(layer, k, bent, rows_in):
        inner(layer, k, bent, rows_in, True)
        rim_tiles(layer, lambda g: jnp.concatenate([bent[k, g, 0:8, :], bent[k, g, ROWS - 8:, :]], axis=0))

    def finish_early(layer, carry):
        s, a = layer // AX, layer % AX
        rim_tiles(layer, lambda g: kept[layer, g])
        for f in range(FIELDS):
            for t in range(1, 7):
                partial[s, f, a, 8 * t:8 * t + 8, :] = partial[s, f, a, 8 * t:8 * t + 8, :] + pitch_fix(s, f, a, t)
        return carry

    def layers(first, last, step):
        products(first, bent_a, rows_a)

        def four_layers(i, carry):
            products(4 * i + 2, bent_b, rows_b)
            step(4 * i, 0, bent_a, rows_a)
            step(4 * i + 1, 1, bent_a, rows_a)
            products(jnp.minimum(4 * i + 4, last - 2), bent_a, rows_a)
            step(4 * i + 2, 0, bent_b, rows_b)
            step(4 * i + 3, 1, bent_b, rows_b)
            return carry

        lax.fori_loop(first // 4, last // 4, four_layers, 0)


    offset = off_ref[0]
    shift, hop = lax.rem(offset, LANES), offset // LANES

    for s in range(2):
        own_rows(s).wait()

    def back_copy(chunk, target, source):
        first, count = CHUNKS[chunk]
        return pltpu.make_async_remote_copy(
            src_ref=outgoing.at[target, :, pl.ds(first, count)], dst_ref=ghost_ref.at[source, :, pl.ds(first, count)],
            send_sem=back_send.at[chunk, target], recv_sem=back_recv.at[chunk, source],
            device_id={"pitch": target}, device_id_type=MESH,
        )

    for chunk, (start, count) in enumerate(CHUNKS):
        done = sum(BEFORE[:chunk])
        if BEFORE[chunk]:
            layers(done, done + BEFORE[chunk], early_layer)

        def turn(source):
            for f in range(start, start + count):
                turned[source, f] = pltpu.roll(planes[1, source, f], shift, 1)

        turn(me)
        for source in sources:
            for s in range(2):
                row_copy(s, chunk, source, source).wait_recv()
            turn(source)

        def forward(f, carry):
            x = []
            for t in range(TILES):
                near = turned[lax.rem(t + 16 - hop, 16), f]
                far = turned[lax.rem(t + 15 - hop, 16), f]
                x.append(jnp.where(lane >= shift, near, far) - planes[0, t, f])
            cs, ss = forward_16(x)
            for c in range(9):
                cosines, sines = twiddle_ref[0, c], twiddle_ref[1, c]
                if c == 0:
                    real, imaginary = cs[0], nothing
                elif c == 8:
                    real, imaginary = cs[8] * cosines, -(cs[8] * sines)
                else:
                    real = cs[c] * cosines - ss[c] * sines
                    imaginary = -(cs[c] * sines + ss[c] * cosines)
                spectrum[c, f, :, 0:LANES] = real
                spectrum[c, f, :, LANES:] = imaginary
            return carry

        lax.fori_loop(start, start + count, forward, 0, unroll=True)
        modes = split_dot(spectrum[:, start:start + count].reshape(72 * count, 256), table_ref)
        modes = modes * blends[:, start:start + count].reshape(72 * count, 256)
        spectrum[:, start:start + count] = split_dot(modes, back_ref).reshape(9, count, 8, 256)

        def inverse(f, carry):
            cs, ss = [], []
            for c in range(9):
                cosines, sines = twiddle_ref[0, c], twiddle_ref[1, c]
                real, imaginary = spectrum[c, f, :, 0:LANES], spectrum[c, f, :, LANES:]
                cs.append(real * cosines - imaginary * sines)
                ss.append(-(real * sines + imaginary * cosines))
            x = inverse_16(cs, ss)
            for t in range(TILES):
                outgoing[t, 0, f] = x[t]
                turned[t, f] = pltpu.roll(x[t], lax.rem(LANES - shift, LANES), 1)
            for t in range(TILES):
                near = turned[lax.rem(t + hop, 16), f]
                far = turned[lax.rem(t + hop + 1, 16), f]
                outgoing[t, 1, f] = jnp.where(lane < LANES - shift, near, far)
            return carry

        lax.fori_loop(start, start + count, inverse, 0, unroll=True)

        for target in targets:
            back_copy(chunk, target, me).start()

    own_back = pltpu.make_async_copy(outgoing.at[me], ghost_ref.at[me], own_sem.at[0])
    own_back.start()

    for copy in (to_above, to_below, to_right, to_left):
        copy.wait()
    keep_low = jnp.where(span == 0, 0.0, 1.0).astype(f32)
    keep_high = jnp.where(span == 7, 0.0, 1.0).astype(f32)
    for s in range(2):

        def unpack(m, carry):
            f, first = m // 4, 4 * (m % 4)
            low = span_recv[0, s, m] * keep_low
            high = span_recv[1, s, m] * keep_high
            for j in range(4):
                cells[s, f, 2 + first + j, 6:8, :] = low[2 * j:2 * j + 2, :]
                cells[s, f, 2 + first + j, 72:74, :] = high[2 * j:2 * j + 2, :]
            return carry

        lax.fori_loop(0, 20, unpack, 0)

        def edges(quarter_pair, carry):
            total = [[None] * FIELDS, [None] * FIELDS]
            for g in range(FIELDS):
                from_left, from_right = pitch_recv[0, s, 2 * g + quarter_pair], pitch_recv[1, s, 2 * g + quarter_pair]
                for half in range(2):
                    if half == 0:
                        halo = jnp.where(group < 2, from_left, pltpu.roll(from_right, 2, 1))
                    else:
                        halo = jnp.where(group < 2, pltpu.roll(from_left, LANES - 2, 1), from_right)
                    plus_1, minus_1 = pltpu.roll(halo, LANES - 1, 1), pltpu.roll(halo, 1, 1)
                    plus_2, minus_2 = pltpu.roll(halo, LANES - 2, 1), pltpu.roll(halo, 2, 1)
                    slope = jnp.where(group == 1, plus_1, jnp.where(group == 2, -minus_1, 0.0))
                    smooth = jnp.where(group < 2, plus_2, minus_2) - 4.0 * jnp.where(
                        group == 1, plus_1, jnp.where(group == 2, minus_1, 0.0)
                    )
                    for f in range(FIELDS):
                        term = weights[(2 * FIELDS + g) * FIELDS + f] * slope
                        if f == g:
                            term = term - scale * smooth
                        total[half][f] = term if total[half][f] is None else total[half][f] + term
            for half in range(2):
                for f in range(FIELDS):
                    edge_fix[s, f, 2 * quarter_pair + half] = total[half][f]
            return carry

        lax.fori_loop(0, 2, edges, 0)

    layers(EARLY, 2 * AX, late_layer)
    lax.fori_loop(0, EARLY, finish_early, 0)

    own_back.wait()

    def finish(j, carry):
        other = lax.rem(me + j, 16)
        for chunk in range(len(CHUNKS)):
            for s in range(2):
                row_copy(s, chunk, other, me).wait_send()
            back_copy(chunk, other, me).wait_send()
            back_copy(chunk, other, other).wait_recv()
        return carry

    lax.fori_loop(1, 16, finish, 0)


def band_table():
    position = np.arange(LANES)
    scale = time_step * damping
    slope = np.zeros((LANES, LANES))
    smooth = np.zeros((LANES, LANES))
    for step, weight in ((1, 1.0), (-1, -1.0)):
        inside = position[(position + step >= 0) & (position + step < LANES)]
        slope[inside + step, inside] += weight
    for step, weight in ((0, 1.0 - 18.0 * scale), (1, 4.0 * scale), (-1, 4.0 * scale), (2, -scale), (-2, -scale)):
        inside = position[(position + step >= 0) & (position + step < LANES)]
        smooth[inside + step, inside] += weight
    table = np.concatenate([slope, smooth], axis=1)
    return np.concatenate([table, table], axis=0).astype(ml_dtypes.bfloat16)


def section(offset, stator, rotor, blend, jacobians, field_mix):
    forward_table, back_table, twiddle = transform_tables()
    whole = pl.BlockSpec(memory_space=pltpu.VMEM)
    anywhere = pl.BlockSpec(memory_space=pl.ANY)
    dma = pltpu.SemaphoreType.DMA
    return pl.pallas_call(
        section_kernel,
        name="section",
        out_shape=(
            pltpu.VMEM((2, FIELDS, AX, ROWS, LANES), f32),
            pltpu.VMEM((16, 2, FIELDS, 8, LANES), f32),
            pltpu.VMEM((75, 8, LANES), f32),
            pltpu.VMEM((25, 8, LANES), f32),
        ),
        in_specs=[pl.BlockSpec(memory_space=pltpu.SMEM)] + [pl.BlockSpec(memory_space=pltpu.HBM)] * 9,
        out_specs=(whole, whole, whole, whole),
        scratch_shapes=[
            pltpu.VMEM((2, FIELDS, AX + 4, ROWS + 16, LANES), f32),
            pltpu.VMEM((2, 16, FIELDS, 8, LANES), f32),
            pltpu.VMEM((9, FIELDS, 8, 256), f32),
            pltpu.VMEM((9, FIELDS, 8, 256), f32),
            pltpu.VMEM((16, FIELDS, 8, LANES), f32),
            pltpu.VMEM((16, 2, FIELDS, 8, LANES), f32),
            pltpu.VMEM((2, 2, 10, 8, LANES), f32),
            pltpu.VMEM((2, 2, 10, 8, LANES), f32),
            pltpu.VMEM((2, 2, 20, 8, LANES), f32),
            pltpu.VMEM((2, 2, 20, 8, LANES), f32),
            pltpu.VMEM((2, FIELDS, ROWS, 256), f32),
            pltpu.VMEM((2, FIELDS, ROWS, 256), f32),
            pltpu.VMEM((2, FIELDS, 24, 256), f32),
            pltpu.VMEM((2, FIELDS, 24, 256), f32),
            pltpu.VMEM((2, FIELDS, 24, 768), f32),
            pltpu.VMEM((EARLY, FIELDS, 16, 256), f32),
            pltpu.VMEM((2, FIELDS, 4, 8, LANES), f32),
            pltpu.VMEM((TILES, 8, LANES), f32),
            pltpu.VMEM((FIELDS, NP), f32),
            pltpu.VMEM((FIELDS, 3, FIELDS), f32),
            pltpu.VMEM((FIELDS, FIELDS), f32),
            pltpu.VMEM((2, 256, 256), bf16),
            pltpu.VMEM((2, 256, 256), bf16),
            pltpu.VMEM((2, 9, 1, LANES), f32),
            pltpu.VMEM((256, 256), bf16),
            dma((2, FIELDS)), dma((2,)), dma((2, len(CHUNKS), 16)), dma((2, len(CHUNKS), 16)), dma((len(CHUNKS), 16)), dma((len(CHUNKS), 16)),
            dma((4,)), dma((4,)), dma((7,)),
        ],
        compiler_params=pltpu.CompilerParams(
            collective_id=0, has_side_effects=True, vmem_limit_bytes=32 << 20
        ),
    )(offset, *(
        pltpu.with_memory_space_constraint(jnp.asarray(x), pltpu.HBM)
        for x in (
            stator, rotor, blend, jacobians.transpose(1, 0, 2), field_mix,
            forward_table, back_table, twiddle, band_table(),
        )
    ))


def close_kernel(partial, ghosts, weights, mixes, st_out, ro_out, ends, store_sem, end_sem):
    outs = (st_out, ro_out)
    scale = time_step * damping
    copies = []
    for s in range(2):
        first = 0 if s == 0 else 2
        for f in range(FIELDS):
            copies.append(pltpu.make_async_copy(
                partial.at[s, f, pl.ds(first, AX - 2)], outs[s].at[f, pl.ds(first, AX - 2)], store_sem.at[s, f]
            ))
    for copy in copies:
        copy.start()

    for s in range(2):

        def fill(block, carry):
            rows = pl.ds(pl.multiple_of(8 * block, 8), 8)
            mixed = []
            for layer in range(2):
                parts = [ghosts[8 * layer + block, s, g] for g in range(FIELDS)]
                found = []
                for f in range(FIELDS):
                    total = mixes[f * FIELDS] * parts[0]
                    for g in range(1, FIELDS):
                        total = total + mixes[f * FIELDS + g] * parts[g]
                    found.append(total if s == 0 else -total)
                mixed.append(found)
            outer, inner = (15, 14) if s == 0 else (0, 1)
            for f in range(FIELDS):
                total = (4.0 * scale) * mixed[0][f] - scale * mixed[1][f]
                for g in range(FIELDS):
                    term = weights[g * FIELDS + f] * mixed[0][g]
                    total = total + term if s == 0 else total - term
                ends[s, f, outer % 2, rows, :] = partial[s, f, outer, rows, :] + total
                ends[s, f, inner % 2, rows, :] = partial[s, f, inner, rows, :] - scale * mixed[0][f]
            return carry

        lax.fori_loop(0, 8, fill, 0)
        last = pltpu.make_async_copy(ends.at[s], outs[s].at[:, pl.ds(14 if s == 0 else 0, 2)], end_sem.at[s])
        last.start()
        copies.append(last)
    for copy in copies:
        copy.wait()


def close(partial, ghosts, weights, mixes):
    anywhere = pl.BlockSpec(memory_space=pl.ANY)
    whole = pl.BlockSpec(memory_space=pltpu.VMEM)
    dma = pltpu.SemaphoreType.DMA
    shape = jax.ShapeDtypeStruct((FIELDS, AX, ROWS, LANES), f32)
    return pl.pallas_call(
        close_kernel,
        name="close",
        out_shape=(shape, shape),
        in_specs=[whole] * 4,
        out_specs=(anywhere, anywhere),
        scratch_shapes=[pltpu.VMEM((2, FIELDS, 2, ROWS, LANES), f32), dma((2, FIELDS)), dma((2,))],
        compiler_params=pltpu.CompilerParams(vmem_limit_bytes=8 << 20),
    )(partial, ghosts, weights, mixes)


def shards(stator_state, rotor_state, jacobians, field_mix, mode_blend, rotor_offset):
    parts = section(rotor_offset, stator_state, rotor_state, mode_blend, jacobians, field_mix)
    return close(*parts)


def solution(mesh):
    in_specs = (P(None, None, "span", "pitch"), P(None, None, "span", "pitch"), P(), P(), P(), P())
    out_specs = (P(None, None, "span", "pitch"), P(None, None, "span", "pitch"))
    return jax.shard_map(shards, mesh=mesh, in_specs=in_specs, out_specs=out_specs, check_vma=False)
```

```python
import math

import jax
import jax.numpy as jnp
import ml_dtypes
import numpy as np
from jax import lax
from jax.experimental import pallas as pl
from jax.experimental.pallas import tpu as pltpu
from jax.sharding import PartitionSpec as P

NP = 2048
FIELDS = 5
AX = 16
ROWS = 64
LANES = 128
TILES = 16
MESH = pl.DeviceIdType.MESH
EARLY = 16
BEFORE = (16,)
CHUNKS = ((0, 5),)
ORDER = (
    (2, 2), (2, 3), (3, 2), (2, 1), (1, 2), (2, 0), (0, 2), (3, 1), (1, 3), (3, 3), (1, 1), (3, 0), (0, 3), (1, 0), (0, 1),
)
f32 = jnp.float32
bf16 = jnp.bfloat16

time_step = 0.5
damping = 1.0 / 32.0


def transform_tables():
    q = np.arange(LANES)
    w = 2.0 * np.pi / LANES

    def cas(m):
        angle = w * (m % LANES)
        return np.cos(angle) + np.sin(angle)

    first, second = np.outer(q, q), np.outer(q, q + 1)
    table = np.block([[cas(first), cas(second)], [-cas(-first), cas(-second)]])

    def parts(array):
        array = array.astype(np.float32)
        high = array.astype(ml_dtypes.bfloat16)
        low = (array - high.astype(np.float32)).astype(ml_dtypes.bfloat16)
        return np.stack([high, low])

    psi = 2.0 * np.pi * np.outer(np.arange(9), q) / NP
    twiddle = np.stack([np.cos(psi), np.sin(psi)]).astype(np.float32)
    return parts(table), parts(table.T / NP), twiddle[:, :, None, :]


def cosine(m):
    return math.cos(2.0 * math.pi * (m % 16) / 16)


def sine(m):
    return math.sin(2.0 * math.pi * (m % 16) / 16)


def weighted(terms):
    total = None
    for weight, value in terms:
        if abs(weight) < 1e-9:
            continue
        if abs(weight - 1.0) < 1e-9:
            total = value if total is None else total + value
        elif abs(weight + 1.0) < 1e-9:
            total = -value if total is None else total - value
        else:
            total = weight * value if total is None else total + weight * value
    return total


def forward_16(x):
    e = [None] + [x[p] + x[16 - p] for p in range(1, 8)]
    o = [None] + [x[p] - x[16 - p] for p in range(1, 8)]
    x_even, x_odd = x[0] + x[8], x[0] - x[8]
    ee = [None] + [e[p] + e[8 - p] for p in range(1, 4)]
    eo = [None] + [e[p] - e[8 - p] for p in range(1, 4)]
    oo = [None] + [o[p] + o[8 - p] for p in range(1, 4)]
    oe = [None] + [o[p] - o[8 - p] for p in range(1, 4)]
    cs, ss = [], []
    for c in range(9):
        if c % 2 == 0:
            cs.append(weighted([(1.0, x_even), (cosine(4 * c), e[4])] + [(cosine(p * c), ee[p]) for p in range(1, 4)]))
            ss.append(weighted([(sine(p * c), oe[p]) for p in range(1, 4)]) if 0 < c < 8 else None)
        else:
            cs.append(weighted([(1.0, x_odd)] + [(cosine(p * c), eo[p]) for p in range(1, 4)]))
            ss.append(weighted([(sine(4 * c), o[4])] + [(sine(p * c), oo[p]) for p in range(1, 4)]))
    return cs, ss


def inverse_16(cs, ss):
    x = [None] * 16
    x[0] = weighted([(1.0, v) for v in cs])
    x[8] = weighted([((-1.0) ** c, v) for c, v in enumerate(cs)])
    for p in range(1, 5):
        ev = weighted([(1.0, cs[0]), (cosine(8 * p), cs[8])] + [(cosine(p * c), cs[c]) for c in range(2, 8, 2)])
        eo = weighted([(cosine(p * c), cs[c]) for c in range(1, 8, 2)])
        ov = weighted([(sine(p * c), ss[c]) for c in range(2, 8, 2)])
        oo = weighted([(sine(p * c), ss[c]) for c in range(1, 8, 2)])
        if p == 4:
            x[4], x[12] = ev + oo, ev - oo
            continue
        x[p] = (ev + eo) + (ov + oo)
        x[16 - p] = (ev + eo) - (ov + oo)
        x[8 - p] = (ev - eo) + (oo - ov)
        x[8 + p] = (ev - eo) - (oo - ov)
    return x


def split_dot(values, table_ref):
    high = values.astype(bf16)
    low = (values - high.astype(f32)).astype(bf16)

    def dot(left, right):
        return jnp.dot(left, right, preferred_element_type=f32)

    return dot(high, table_ref[0]) + dot(low, table_ref[0]) + dot(high, table_ref[1])


def section_kernel(
    off_ref, st_ref, ro_ref, blend_hbm, jac_hbm, mix_hbm, table_hbm, back_hbm, twiddle_hbm, band_hbm,
    partial, ghost_ref, weights, mixes,
    cells, planes, spectrum, blends, turned, outgoing, pitch_pack, pitch_recv, span_pack, span_recv,
    bent_a, bent_b, rows_a, rows_b, radial, kept, edge_fix, permuted, blend_v, jac_v, mix_v, table_ref, back_ref, twiddle_ref, band_ref,
    load_sem, own_sem, row_send, row_recv, back_send, back_recv, halo_send, halo_recv, small_sem,
):
    me = lax.axis_index("pitch")
    span = lax.axis_index("span")
    left, right = lax.rem(me + 15, 16), lax.rem(me + 1, 16)
    targets = [4 * lax.rem(me // 4 + dx, 4) + lax.rem(me + dz, 4) for dx, dz in ORDER]
    sources = [4 * lax.rem(me // 4 + 4 - dx, 4) + lax.rem(me + 4 - dz, 4) for dx, dz in ORDER]
    below, above = lax.rem(span + 7, 8), lax.rem(span + 1, 8)
    states = (st_ref, ro_ref)

    def load(s, f):
        return pltpu.make_async_copy(states[s].at[f], cells.at[s, f, pl.ds(2, AX), pl.ds(8, ROWS)], load_sem.at[s, f])

    def row_block(s, target, first=0, count=FIELDS):
        layer, block = target // 8, target % 8
        axial = 15 - layer if s == 0 else layer
        rows = pl.ds(pl.multiple_of(8 * block, 8), 8)
        return states[s].at[pl.ds(first, count), axial, rows, :]

    def own_rows(s):
        return pltpu.make_async_copy(row_block(s, me), planes.at[s, me], own_sem.at[s])

    barrier = pltpu.get_barrier_semaphore()

    def greet(j, carry):
        pl.semaphore_signal(barrier, inc=1, device_id={"pitch": lax.rem(me + j, 16)}, device_id_type=MESH)
        return carry

    lax.fori_loop(1, 16, greet, 0)
    for other in (below, above):
        pl.semaphore_signal(barrier, inc=1, device_id={"span": other}, device_id_type=MESH)

    smalls = [
        pltpu.make_async_copy(source, target, small_sem.at[i])
        for i, (source, target) in enumerate((
            (blend_hbm, blend_v), (jac_hbm, jac_v), (mix_hbm, mix_v),
            (table_hbm, table_ref), (back_hbm, back_ref), (twiddle_hbm, twiddle_ref), (band_hbm, band_ref),
        ))
    ]
    for s in range(2):
        own_rows(s).start()
    for s in range(2):
        for f in range(FIELDS):
            load(s, f).start()
    for copy in smalls:
        copy.start()

    lane = lax.broadcasted_iota(jnp.int32, (8, LANES), 1)
    row = lax.broadcasted_iota(jnp.int32, (8, LANES), 0)
    group = lane % 4
    nothing = jnp.zeros((8, LANES), f32)
    scale = time_step * damping
    for s in range(2):
        for f in range(FIELDS):
            for t in range(8):
                for a in (0, 1, 18, 19):
                    cells[s, f, a, 8 + 8 * t:16 + 8 * t, :] = nothing

    for copy in smalls:
        copy.wait()
    for d in range(3):
        for f in range(FIELDS):
            for g in range(FIELDS):
                value = jnp.broadcast_to(jac_v[f, d:d + 1, g:g + 1], (8, LANES))
                weights[(d * FIELDS + g) * FIELDS + f] = (-0.5 * time_step) * value
    for f in range(FIELDS):
        for g in range(FIELDS):
            mixes[f * FIELDS + g] = jnp.broadcast_to(mix_v[f:f + 1, g:g + 1], (8, LANES))

    spot = lax.broadcasted_iota(jnp.int32, (24, 256), 1)
    field = sum((spot >= 48 * g).astype(jnp.int32) for g in range(1, FIELDS + 1))
    place = spot - 48 * field
    for block in range(2):
        step = place - lax.broadcasted_iota(jnp.int32, (24, 256), 0) - (8 + 8 * block)
        side = (step == 1).astype(f32) - (step == -1).astype(f32)
        blur = (4.0 * scale) * (jnp.abs(step) == 1).astype(f32) - scale * (jnp.abs(step) == 2).astype(f32)
        for f in range(FIELDS):
            value = jnp.where(field == f, blur, 0.0)
            for g in range(FIELDS):
                weight = jnp.broadcast_to(weights[(FIELDS + g) * FIELDS + f][0:1, 0:1], (24, 256))
                value = value + jnp.where(field == g, weight * side, 0.0)
            high = value.astype(bf16).astype(f32)
            low = value - high
            radial[block, f] = jnp.concatenate([high, low, high], axis=1)

    spare = jnp.zeros((3, LANES), f32)
    blend_rows = jnp.concatenate(
        [part for t in range(TILES) for part in (blend_v[:, LANES * t:LANES * t + LANES], spare)], axis=0
    )
    source_lane = lax.broadcasted_iota(jnp.int32, (LANES, LANES), 0)
    target_lane = lax.broadcasted_iota(jnp.int32, (LANES, LANES), 1)
    chosen = (8 * (source_lane % 16) + source_lane // 16 == target_lane).astype(f32)
    permuted[...] = jnp.dot(
        blend_rows, chosen, precision=lax.Precision.HIGHEST, preferred_element_type=f32
    ).reshape(TILES, 8, LANES)

    def mode_row(k):
        total = nothing
        for t in range(TILES):
            shift = (8 * (t - k)) % LANES
            value = permuted[t]
            total = jnp.where(lane // 8 == t, pltpu.roll(value, shift, 1) if shift else value, total)
        return total

    for c in range(9):
        near = mode_row(c)
        other = mode_row(16 - c) if 0 < c < 8 else nothing
        for f in range(FIELDS):
            blends[c, f, :, 0:LANES] = jnp.broadcast_to(near[f:f + 1, :], (8, LANES))
            blends[c, f, :, LANES:] = jnp.broadcast_to(other[f:f + 1, :], (8, LANES))

    pl.semaphore_wait(barrier, 17)

    def row_copy(s, chunk, target, source):
        first, count = CHUNKS[chunk]
        return pltpu.make_async_remote_copy(
            src_ref=row_block(s, target, first, count), dst_ref=planes.at[s, source, pl.ds(first, count)],
            send_sem=row_send.at[s, chunk, target], recv_sem=row_recv.at[s, chunk, source],
            device_id={"pitch": target}, device_id_type=MESH,
        )

    for chunk in range(len(CHUNKS)):

        for target in targets:
            for s in range(2):
                row_copy(s, chunk, target, me).start()

    def halo_copy(slot, src, dst, where):
        return pltpu.make_async_remote_copy(
            src_ref=src, dst_ref=dst, send_sem=halo_send.at[slot], recv_sem=halo_recv.at[slot],
            device_id=where, device_id_type=MESH,
        )

    to_above = halo_copy(0, span_pack.at[0], span_recv.at[0], {"span": above})
    to_below = halo_copy(1, span_pack.at[1], span_recv.at[1], {"span": below})
    to_right = halo_copy(2, pitch_pack.at[0], pitch_recv.at[0], {"pitch": right})
    to_left = halo_copy(3, pitch_pack.at[1], pitch_recv.at[1], {"pitch": left})

    for s in range(2):
        for f in range(FIELDS):
            load(s, f).wait()

        def pack(pair, carry):
            found = []
            for half in range(2):
                m = 2 * pair + half
                f, first = m // 4, 2 + 4 * (m % 4)
                edge = jnp.zeros((8, LANES), f32)
                low = jnp.zeros((8, LANES), f32)
                high = jnp.zeros((8, LANES), f32)
                for j in range(4):
                    for t in range(8):
                        n = 8 * j + t
                        value = cells[s, f, first + j, 8 + 8 * t:16 + 8 * t, :]
                        edge = jnp.where(lane // 4 == n, pltpu.roll(value, (2 + 4 * n) % LANES, 1), edge)
                        if t == 0:
                            low = jnp.where(row // 2 == j, pltpu.roll(value, 2 * j, 0) if j else value, low)
                        if t == 7:
                            shift = (2 * j + 2) % 8
                            high = jnp.where(row // 2 == j, pltpu.roll(value, shift, 0) if shift else value, high)
                span_pack[0, s, m] = high
                span_pack[1, s, m] = low
                found.append(edge)
            pitch_pack[0, s, pair] = jnp.where(group < 2, found[0], pltpu.roll(found[1], 2, 1))
            pitch_pack[1, s, pair] = jnp.where(group < 2, pltpu.roll(found[0], LANES - 2, 1), found[1])
            return carry

        lax.fori_loop(0, 10, pack, 0)
    for copy in (to_above, to_below, to_right, to_left):
        copy.start()

    def base_ghosts(block, carry):
        rows = pl.ds(pl.multiple_of(8 + 8 * block, 8), 8)
        for s in range(2):
            for layer in range(2):
                kept = [cells[s, g, 17 - layer if s == 0 else 2 + layer, rows, :] for g in range(FIELDS)]
                for f in range(FIELDS):
                    total = mixes[f * FIELDS] * kept[0]
                    for g in range(1, FIELDS):
                        total = total + mixes[f * FIELDS + g] * kept[g]
                    cells[s, f, 18 + layer if s == 0 else 1 - layer, rows, :] = total
        return carry

    lax.fori_loop(0, 8, base_ghosts, 0)

    rim = (lane < 2) | (lane >= LANES - 2)

    def products(layer, bent, rows_out):
        highs, lows = [], []
        for k in range(2):
            s, a = (layer + k) // AX, (layer + k) % AX
            values = cells[s, :, a + 2, 8:8 + ROWS, :].reshape(FIELDS * ROWS, LANES)
            high = values.astype(bf16)
            low = (values - high.astype(f32)).astype(bf16)
            both = jnp.concatenate([high, low], axis=1)
            bent[k] = jnp.dot(both, band_ref[...], preferred_element_type=f32).reshape(FIELDS, ROWS, 256)
            highs.append(high)
            lows.append(low)
        blank = jnp.zeros((16, LANES), bf16)
        for block in range(2):

            def stacked(parts):
                return jnp.concatenate([
                    jnp.concatenate(
                        [part[ROWS * g + 16 * block:ROWS * g + 16 * block + 48, :] for g in range(FIELDS)] + [blank], axis=0
                    )
                    for part in parts
                ], axis=1)

            upper = stacked(highs)
            data = jnp.concatenate([upper, upper, stacked(lows)], axis=0)
            left = radial[block].reshape(FIELDS * 24, 768).astype(bf16)
            rows_out[block] = jnp.dot(left, data, preferred_element_type=f32).reshape(FIELDS, 24, 256)

    def pitch_fix(s, f, a, tile):
        amount = lax.rem(126 - 32 * lax.rem(a, 4) - 4 * tile + 2 * LANES, LANES)
        return jnp.where(rim, pltpu.roll(edge_fix[s, f, a // 4], amount, 1), 0.0)

    def rim_tiles(layer, bent):
        s, a = layer // AX, layer % AX
        sums = [None] * FIELDS
        for g in range(FIELDS):

            def get(axial, radial):
                low, high = 8 + radial, ROWS + radial
                return jnp.stack([
                    cells[s, g, a + 2 + axial, low:low + 8, :], cells[s, g, a + 2 + axial, high:high + 8, :],
                ])

            ahead, behind = get(1, 0), get(-1, 0)
            up, down = get(0, 1), get(0, -1)
            near = (ahead + behind) + (up + down)
            far = (get(2, 0) + get(-2, 0)) + (get(0, 2) + get(0, -2))
            pitch = bent(g)
            along = pitch[:, 0:LANES].reshape(2, 8, LANES)
            own = pitch[:, LANES:].reshape(2, 8, LANES) + ((4.0 * scale) * near - scale * far)
            own = own + jnp.stack([pitch_fix(s, g, a, 0), pitch_fix(s, g, a, 7)])
            sums[g] = own if sums[g] is None else sums[g] + own
            for d, slope in enumerate((ahead - behind, up - down, along)):
                for f in range(FIELDS):
                    term = weights[(d * FIELDS + g) * FIELDS + f] * slope
                    sums[f] = term if sums[f] is None else sums[f] + term
        for f in range(FIELDS):
            partial[s, f, a, 0:8, :] = sums[f][0]
            partial[s, f, a, ROWS - 8:ROWS, :] = sums[f][1]

    def inner(layer, k, bent, rows_in, fixed):
        s, a = layer // AX, layer % AX
        sums = [
            jnp.concatenate([rows_in[block, f, :, LANES * k:LANES * k + LANES] for block in range(2)], axis=0).reshape(6, 8, LANES)
            for f in range(FIELDS)
        ]
        for g in range(FIELDS):

            def get(axial):
                return cells[s, g, a + 2 + axial, 16:8 + ROWS - 8, :].reshape(6, 8, LANES)

            ahead, behind = get(1), get(-1)
            along = bent[k, g, 8:ROWS - 8, 0:LANES].reshape(6, 8, LANES)
            own = bent[k, g, 8:ROWS - 8, LANES:].reshape(6, 8, LANES)
            own = own + ((4.0 * scale) * (ahead + behind) - scale * (get(2) + get(-2)))
            if fixed:
                own = own + jnp.stack([pitch_fix(s, g, a, 1 + t) for t in range(6)])
            sums[g] = sums[g] + own
            for d, slope in ((0, ahead - behind), (2, along)):
                for f in range(FIELDS):
                    sums[f] = sums[f] + weights[(d * FIELDS + g) * FIELDS + f] * slope
        for f in range(FIELDS):
            partial[s, f, a, 8:ROWS - 8, :] = sums[f].reshape(48, LANES)

    def early_layer(layer, k, bent, rows_in):
        inner(layer, k, bent, rows_in, False)
        kept[layer, :, 0:8, :] = bent[k, :, 0:8, :]
        kept[layer, :, 8:16, :] = bent[k, :, ROWS - 8:, :]

    def late_layer(layer, k, bent, rows_in):
        inner(layer, k, bent, rows_in, True)
        rim_tiles(layer, lambda g: jnp.concatenate([bent[k, g, 0:8, :], bent[k, g, ROWS - 8:, :]], axis=0))

    def finish_early(layer, carry):
        s, a = layer // AX, layer % AX
        rim_tiles(layer, lambda g: kept[layer, g])
        for f in range(FIELDS):
            for t in range(1, 7):
                partial[s, f, a, 8 * t:8 * t + 8, :] = partial[s, f, a, 8 * t:8 * t + 8, :] + pitch_fix(s, f, a, t)
        return carry

    def layers(first, last, step):
        products(first, bent_a, rows_a)

        def four_layers(i, carry):
            products(4 * i + 2, bent_b, rows_b)
            step(4 * i, 0, bent_a, rows_a)
            step(4 * i + 1, 1, bent_a, rows_a)
            products(jnp.minimum(4 * i + 4, last - 2), bent_a, rows_a)
            step(4 * i + 2, 0, bent_b, rows_b)
            step(4 * i + 3, 1, bent_b, rows_b)
            return carry

        lax.fori_loop(first // 4, last // 4, four_layers, 0)


    offset = off_ref[0]
    shift, hop = lax.rem(offset, LANES), offset // LANES

    for s in range(2):
        own_rows(s).wait()

    def back_copy(chunk, target, source):
        first, count = CHUNKS[chunk]
        return pltpu.make_async_remote_copy(
            src_ref=outgoing.at[target, :, pl.ds(first, count)], dst_ref=ghost_ref.at[source, :, pl.ds(first, count)],
            send_sem=back_send.at[chunk, target], recv_sem=back_recv.at[chunk, source],
            device_id={"pitch": target}, device_id_type=MESH,
        )

    for chunk, (start, count) in enumerate(CHUNKS):
        done = sum(BEFORE[:chunk])
        if BEFORE[chunk]:
            layers(done, done + BEFORE[chunk], early_layer)

        def turn(source):
            for f in range(start, start + count):
                turned[source, f] = pltpu.roll(planes[1, source, f], shift, 1)

        turn(me)
        for source in sources:
            for s in range(2):
                row_copy(s, chunk, source, source).wait_recv()
            turn(source)

        def forward(f, carry):
            x = []
            for t in range(TILES):
                near = turned[lax.rem(t + 16 - hop, 16), f]
                far = turned[lax.rem(t + 15 - hop, 16), f]
                x.append(jnp.where(lane >= shift, near, far) - planes[0, t, f])
            cs, ss = forward_16(x)
            for c in range(9):
                cosines, sines = twiddle_ref[0, c], twiddle_ref[1, c]
                if c == 0:
                    real, imaginary = cs[0], nothing
                elif c == 8:
                    real, imaginary = cs[8] * cosines, -(cs[8] * sines)
                else:
                    real = cs[c] * cosines - ss[c] * sines
                    imaginary = -(cs[c] * sines + ss[c] * cosines)
                spectrum[c, f, :, 0:LANES] = real
                spectrum[c, f, :, LANES:] = imaginary
            return carry

        lax.fori_loop(start, start + count, forward, 0, unroll=True)
        modes = split_dot(spectrum[:, start:start + count].reshape(72 * count, 256), table_ref)
        modes = modes * blends[:, start:start + count].reshape(72 * count, 256)
        spectrum[:, start:start + count] = split_dot(modes, back_ref).reshape(9, count, 8, 256)

        def inverse(f, carry):
            cs, ss = [], []
            for c in range(9):
                cosines, sines = twiddle_ref[0, c], twiddle_ref[1, c]
                real, imaginary = spectrum[c, f, :, 0:LANES], spectrum[c, f, :, LANES:]
                cs.append(real * cosines - imaginary * sines)
                ss.append(-(real * sines + imaginary * cosines))
            x = inverse_16(cs, ss)
            for t in range(TILES):
                outgoing[t, 0, f] = x[t]
                turned[t, f] = pltpu.roll(x[t], lax.rem(LANES - shift, LANES), 1)
            for t in range(TILES):
                near = turned[lax.rem(t + hop, 16), f]
                far = turned[lax.rem(t + hop + 1, 16), f]
                outgoing[t, 1, f] = jnp.where(lane < LANES - shift, near, far)
            return carry

        lax.fori_loop(start, start + count, inverse, 0, unroll=True)

        for target in targets:
            back_copy(chunk, target, me).start()

    own_back = pltpu.make_async_copy(outgoing.at[me], ghost_ref.at[me], own_sem.at[0])
    own_back.start()

    for copy in (to_above, to_below, to_right, to_left):
        copy.wait()
    keep_low = jnp.where(span == 0, 0.0, 1.0).astype(f32)
    keep_high = jnp.where(span == 7, 0.0, 1.0).astype(f32)
    for s in range(2):

        def unpack(m, carry):
            f, first = m // 4, 4 * (m % 4)
            low = span_recv[0, s, m] * keep_low
            high = span_recv[1, s, m] * keep_high
            for j in range(4):
                cells[s, f, 2 + first + j, 6:8, :] = low[2 * j:2 * j + 2, :]
                cells[s, f, 2 + first + j, 72:74, :] = high[2 * j:2 * j + 2, :]
            return carry

        lax.fori_loop(0, 20, unpack, 0)

        def edges(quarter_pair, carry):
            total = [[None] * FIELDS, [None] * FIELDS]
            for g in range(FIELDS):
                from_left, from_right = pitch_recv[0, s, 2 * g + quarter_pair], pitch_recv[1, s, 2 * g + quarter_pair]
                for half in range(2):
                    if half == 0:
                        halo = jnp.where(group < 2, from_left, pltpu.roll(from_right, 2, 1))
                    else:
                        halo = jnp.where(group < 2, pltpu.roll(from_left, LANES - 2, 1), from_right)
                    plus_1, minus_1 = pltpu.roll(halo, LANES - 1, 1), pltpu.roll(halo, 1, 1)
                    plus_2, minus_2 = pltpu.roll(halo, LANES - 2, 1), pltpu.roll(halo, 2, 1)
                    slope = jnp.where(group == 1, plus_1, jnp.where(group == 2, -minus_1, 0.0))
                    smooth = jnp.where(group < 2, plus_2, minus_2) - 4.0 * jnp.where(
                        group == 1, plus_1, jnp.where(group == 2, minus_1, 0.0)
                    )
                    for f in range(FIELDS):
                        term = weights[(2 * FIELDS + g) * FIELDS + f] * slope
                        if f == g:
                            term = term - scale * smooth
                        total[half][f] = term if total[half][f] is None else total[half][f] + term
            for half in range(2):
                for f in range(FIELDS):
                    edge_fix[s, f, 2 * quarter_pair + half] = total[half][f]
            return carry

        lax.fori_loop(0, 2, edges, 0)

    layers(EARLY, 2 * AX, late_layer)
    lax.fori_loop(0, EARLY, finish_early, 0)

    own_back.wait()

    def finish(j, carry):
        other = lax.rem(me + j, 16)
        for chunk in range(len(CHUNKS)):
            for s in range(2):
                row_copy(s, chunk, other, me).wait_send()
            back_copy(chunk, other, me).wait_send()
            back_copy(chunk, other, other).wait_recv()
        return carry

    lax.fori_loop(1, 16, finish, 0)


def band_table():
    position = np.arange(LANES)
    scale = time_step * damping
    slope = np.zeros((LANES, LANES))
    smooth = np.zeros((LANES, LANES))
    for step, weight in ((1, 1.0), (-1, -1.0)):
        inside = position[(position + step >= 0) & (position + step < LANES)]
        slope[inside + step, inside] += weight
    for step, weight in ((0, 1.0 - 18.0 * scale), (1, 4.0 * scale), (-1, 4.0 * scale), (2, -scale), (-2, -scale)):
        inside = position[(position + step >= 0) & (position + step < LANES)]
        smooth[inside + step, inside] += weight
    table = np.concatenate([slope, smooth], axis=1)
    return np.concatenate([table, table], axis=0).astype(ml_dtypes.bfloat16)


def section(offset, stator, rotor, blend, jacobians, field_mix):
    forward_table, back_table, twiddle = transform_tables()
    whole = pl.BlockSpec(memory_space=pltpu.VMEM)
    anywhere = pl.BlockSpec(memory_space=pl.ANY)
    dma = pltpu.SemaphoreType.DMA
    return pl.pallas_call(
        section_kernel,
        name="section",
        out_shape=(
            pltpu.VMEM((2, FIELDS, AX, ROWS, LANES), f32),
            pltpu.VMEM((16, 2, FIELDS, 8, LANES), f32),
            pltpu.VMEM((75, 8, LANES), f32),
            pltpu.VMEM((25, 8, LANES), f32),
        ),
        in_specs=[pl.BlockSpec(memory_space=pltpu.SMEM)] + [pl.BlockSpec(memory_space=pltpu.HBM)] * 9,
        out_specs=(whole, whole, whole, whole),
        scratch_shapes=[
            pltpu.VMEM((2, FIELDS, AX + 4, ROWS + 16, LANES), f32),
            pltpu.VMEM((2, 16, FIELDS, 8, LANES), f32),
            pltpu.VMEM((9, FIELDS, 8, 256), f32),
            pltpu.VMEM((9, FIELDS, 8, 256), f32),
            pltpu.VMEM((16, FIELDS, 8, LANES), f32),
            pltpu.VMEM((16, 2, FIELDS, 8, LANES), f32),
            pltpu.VMEM((2, 2, 10, 8, LANES), f32),
            pltpu.VMEM((2, 2, 10, 8, LANES), f32),
            pltpu.VMEM((2, 2, 20, 8, LANES), f32),
            pltpu.VMEM((2, 2, 20, 8, LANES), f32),
            pltpu.VMEM((2, FIELDS, ROWS, 256), f32),
            pltpu.VMEM((2, FIELDS, ROWS, 256), f32),
            pltpu.VMEM((2, FIELDS, 24, 256), f32),
            pltpu.VMEM((2, FIELDS, 24, 256), f32),
            pltpu.VMEM((2, FIELDS, 24, 768), f32),
            pltpu.VMEM((EARLY, FIELDS, 16, 256), f32),
            pltpu.VMEM((2, FIELDS, 4, 8, LANES), f32),
            pltpu.VMEM((TILES, 8, LANES), f32),
            pltpu.VMEM((FIELDS, NP), f32),
            pltpu.VMEM((FIELDS, 3, FIELDS), f32),
            pltpu.VMEM((FIELDS, FIELDS), f32),
            pltpu.VMEM((2, 256, 256), bf16),
            pltpu.VMEM((2, 256, 256), bf16),
            pltpu.VMEM((2, 9, 1, LANES), f32),
            pltpu.VMEM((256, 256), bf16),
            dma((2, FIELDS)), dma((2,)), dma((2, len(CHUNKS), 16)), dma((2, len(CHUNKS), 16)), dma((len(CHUNKS), 16)), dma((len(CHUNKS), 16)),
            dma((4,)), dma((4,)), dma((7,)),
        ],
        compiler_params=pltpu.CompilerParams(
            collective_id=0, has_side_effects=True, vmem_limit_bytes=32 << 20
        ),
    )(offset, *(
        pltpu.with_memory_space_constraint(jnp.asarray(x), pltpu.HBM)
        for x in (
            stator, rotor, blend, jacobians.transpose(1, 0, 2), field_mix,
            forward_table, back_table, twiddle, band_table(),
        )
    ))


def close_kernel(partial, ghosts, weights, mixes, st_out, ro_out, ends, store_sem, end_sem):
    outs = (st_out, ro_out)
    scale = time_step * damping
    copies = []
    for s in range(2):
        first = 0 if s == 0 else 2
        for f in range(FIELDS):
            copies.append(pltpu.make_async_copy(
                partial.at[s, f, pl.ds(first, AX - 2)], outs[s].at[f, pl.ds(first, AX - 2)], store_sem.at[s, f]
            ))
    for copy in copies:
        copy.start()

    for s in range(2):

        def fill(block, carry):
            rows = pl.ds(pl.multiple_of(8 * block, 8), 8)
            mixed = []
            for layer in range(2):
                parts = [ghosts[8 * layer + block, s, g] for g in range(FIELDS)]
                found = []
                for f in range(FIELDS):
                    total = mixes[f * FIELDS] * parts[0]
                    for g in range(1, FIELDS):
                        total = total + mixes[f * FIELDS + g] * parts[g]
                    found.append(total if s == 0 else -total)
                mixed.append(found)
            outer, inner = (15, 14) if s == 0 else (0, 1)
            for f in range(FIELDS):
                total = (4.0 * scale) * mixed[0][f] - scale * mixed[1][f]
                for g in range(FIELDS):
                    term = weights[g * FIELDS + f] * mixed[0][g]
                    total = total + term if s == 0 else total - term
                ends[s, f, outer % 2, rows, :] = partial[s, f, outer, rows, :] + total
                ends[s, f, inner % 2, rows, :] = partial[s, f, inner, rows, :] - scale * mixed[0][f]
            return carry

        lax.fori_loop(0, 8, fill, 0)
        last = pltpu.make_async_copy(ends.at[s], outs[s].at[:, pl.ds(14 if s == 0 else 0, 2)], end_sem.at[s])
        last.start()
        copies.append(last)
    for copy in copies:
        copy.wait()


def close(partial, ghosts, weights, mixes):
    anywhere = pl.BlockSpec(memory_space=pl.ANY)
    whole = pl.BlockSpec(memory_space=pltpu.VMEM)
    dma = pltpu.SemaphoreType.DMA
    shape = jax.ShapeDtypeStruct((FIELDS, AX, ROWS, LANES), f32)
    return pl.pallas_call(
        close_kernel,
        name="close",
        out_shape=(shape, shape),
        in_specs=[whole] * 4,
        out_specs=(anywhere, anywhere),
        scratch_shapes=[pltpu.VMEM((2, FIELDS, 2, ROWS, LANES), f32), dma((2, FIELDS)), dma((2,))],
        compiler_params=pltpu.CompilerParams(vmem_limit_bytes=8 << 20),
    )(partial, ghosts, weights, mixes)


def shards(stator_state, rotor_state, jacobians, field_mix, mode_blend, rotor_offset):
    parts = section(rotor_offset, stator_state, rotor_state, mode_blend, jacobians, field_mix)
    return close(*parts)


def solution(mesh):
    in_specs = (P(None, None, "span", "pitch"), P(None, None, "span", "pitch"), P(), P(), P(), P())
    out_specs = (P(None, None, "span", "pitch"), P(None, None, "span", "pitch"))
    return jax.shard_map(shards, mesh=mesh, in_specs=in_specs, out_specs=out_specs, check_vma=False)
```
